32 devices in a mesh: groups: 2 (over x), tile: 4 (over y, core), sect: 4 (over z).
Axes of the slice: x: 2, y: 2, z: 4, core: 2. Of those that a mesh axis runs over, the one named last changes fastest.
Arguments:
- source_probes: float32 [2, 32, 8192], P(None, 'groups', ('tile', 'sect')), parts along dimension 1, may hold values from -6 to 6
- near_blocks: bfloat16 [4, 9, 512, 8192], P('groups', None, None, ('tile', 'sect')), parts along dimension 0, may hold values from -0.0625 to 0.0625
- bloch_angle: float32 [4], P('groups'), parts along dimension 0, may hold values from -3.140625 to 3.140625
- grid_row: int32 [8192], P(('tile', 'sect')), may hold values from 0 to 511, as said below
- grid_col: int32 [8192], P(('tile', 'sect')), may hold values from 0 to 511, as said below
- stencil: bfloat16 [4, 4, 8192], P(None, None, ('tile', 'sect')), may hold values from 0.19921875 to 1
- recip_kernel: float32 [1024, 512], P('groups', ('tile', 'sect')), parts along dimension 0, may hold values from 0.1 to 2
Outputs:
- first_image: float32 [2, 32, 8192], P(None, 'groups', ('tile', 'sect')), parts along dimension 1
- second_image: float32 [2, 32, 8192], P(None, 'groups', ('tile', 'sect')), parts along dimension 1
The draws below stay inside these ranges and needn't reach their ends.
There are 2 independent parts, one for each index of `groups`. The reference program is written for one: setup_inputs(seed, part) draws one part's arguments, and reference() takes and returns one part's arrays. A program takes and returns all parts, laid end to end along the dimension named above; an argument that names none is the same for every part. Nothing has to cross between parts.
Inputs may be any that keep to these rules, and one draw needn't show every extreme that they name: `grid_row`: panel i has its first stencil row among the 32 grid rows (i // 512) * 32 to (i // 512 + 1) * 32 - 1, and every grid row is the first row of some panel. `grid_col`: every grid column is the first column of some panel.
All inputs are finite; a program needn't handle non-finite values.
Results may differ from the reference program's by a relative error of at most 0.0032.
Values may be sent and summed in bfloat16 or wider, within the bound.
A program may use at most 128 MiB of HBM per device.

```python
import math
import jax
import jax.numpy as jnp
from jax import lax

PB = 512
PROBES = 16
STENCIL = 4
NG1 = 512
NG2 = 512
PANELS = 8192
ROWS_DEV = 32
N_TILE = 4
N_SECT = 4


def draw_grid_row(key, part):

    def one_block(block):
        block_key = jax.random.fold_in(key, block)
        order_key, random_key = jax.random.split(block_key)
        shuffled = jax.random.permutation(order_key, PB)
        random_rows = jax.random.randint(random_key, (PB,), 0, ROWS_DEV)
        within_rows = jnp.where(shuffled < ROWS_DEV, shuffled, random_rows)
        return block * ROWS_DEV + within_rows
    blocks = jnp.arange(PANELS // PB, dtype=jnp.int32)
    return jax.vmap(one_block)(blocks).reshape(PANELS).astype(jnp.int32)


def draw_grid_col(key, part):
    shuffled = jax.random.permutation(jax.random.fold_in(key, 7), PANELS)
    return (shuffled % NG2).astype(jnp.int32)


def block_levels(rng, dims, shards, low, high):
    factor_of, own = 1.0, jax.random.fold_in(rng, 6)
    for dim, shards_of in shards:
        heights = jnp.exp(jax.random.uniform(jax.random.fold_in(own, dim), (shards_of,), jnp.float32, low / len(shards), high / len(shards)))
        factor_of = factor_of * jnp.repeat(heights, dims[dim] // shards_of).reshape([-1 if axis == dim else 1 for axis in range(len(dims))])
    return factor_of


def scatter_about(key, dims, width, most, shards=(), held_as=jnp.bfloat16):
    drawn = jax.random.normal(key, dims, jnp.float32) * width
    if len(shards) > 0:
        drawn = block_levels(key, dims, shards, -0.22, 0.18) * drawn
    return jnp.clip(drawn, min=-most, max=most).astype(held_as)


def setup_inputs(seed: int = 0, part: int = 0) -> dict:
    key_of = jax.random.split(jax.random.key(seed), 8)
    part_splits = jax.random.split(jax.random.fold_in(key_of[7], part), 8)
    source_probes = scatter_about(part_splits[0], (2, PROBES, PANELS), 1.0, 6.0, ((2, 16),), jnp.float32)
    near_blocks = scatter_about(part_splits[1], (2, 9, PB, PANELS), (18 * PB) ** -0.5, 0.0625, ((3, 16),))
    bloch_angle = jnp.clip(jax.random.uniform(part_splits[2], (2,), jnp.float32, -3.140625, 3.140625), -3.140625, 3.140625)
    grid_row = draw_grid_row(jax.random.fold_in(key_of[7], 71), part)
    grid_col = draw_grid_col(jax.random.fold_in(key_of[7], 71), part)
    stencil = jnp.clip(0.19921875 + 0.80078125 * jax.random.uniform(key_of[5], (STENCIL, STENCIL, PANELS), jnp.float32) ** block_levels(key_of[5], (STENCIL, STENCIL, PANELS), ((2, 16),), -0.2, 0.2), 0.19921875, 1.0).astype(jnp.bfloat16)
    recip_kernel = jnp.clip(jnp.exp(math.log(2.0) - 2.9957323 * jax.random.uniform(part_splits[6], (NG1, NG2), jnp.float32) ** block_levels(part_splits[6], (NG1, NG2), ((1, 16),), -0.2, 0.2)), 0.1, 2.0)
    return dict(source_probes=source_probes, near_blocks=near_blocks, bloch_angle=bloch_angle, grid_row=grid_row, grid_col=grid_col, stencil=stencil, recip_kernel=recip_kernel)


def near_apply(rounded, near_blocks, bloch_angle):
    blocks = rounded.reshape(2, PROBES, N_TILE, N_SECT, PB)
    weights = near_blocks.reshape(2, 9, PB, N_TILE, N_SECT, PB)
    tile_ids = jnp.arange(N_TILE)
    sect_ids = jnp.arange(N_SECT)
    total_real = jnp.zeros((PROBES, N_TILE, N_SECT, PB), jnp.float32)
    total_imag = jnp.zeros((PROBES, N_TILE, N_SECT, PB), jnp.float32)
    for tile_off in (-1, 0, 1):
        for sect_off in (-1, 0, 1):
            index = (tile_off + 1) * 3 + sect_off + 1
            shifted = jnp.roll(blocks, (-tile_off, -sect_off), axis=(2, 3))
            with_real = jnp.einsum("cptsj,jtsi->cptsi", shifted, weights[0, index].astype(jnp.float32))
            with_imag = jnp.einsum("cptsj,jtsi->cptsi", shifted, weights[1, index].astype(jnp.float32))
            part_real = with_real[0] - with_imag[1]
            part_imag = with_real[1] + with_imag[0]
            if tile_off != 0 or sect_off != 0:
                angle_tile = jnp.zeros((N_TILE,), jnp.float32)
                angle_sect = jnp.zeros((N_SECT,), jnp.float32)
                if tile_off != 0:
                    border = tile_ids == (N_TILE - 1 if tile_off == 1 else 0)
                    angle_tile = jnp.where(border, bloch_angle[0] * tile_off, 0.0)
                if sect_off != 0:
                    border = sect_ids == (N_SECT - 1 if sect_off == 1 else 0)
                    angle_sect = jnp.where(border, bloch_angle[1] * sect_off, 0.0)
                phase_angle = angle_tile[:, None] + angle_sect[None, :]
                cos_part = jnp.cos(phase_angle)[None, :, :, None]
                sin_part = jnp.sin(phase_angle)[None, :, :, None]
                part_real, part_imag = part_real * cos_part - part_imag * sin_part, part_real * sin_part + part_imag * cos_part
            total_real = total_real + part_real
            total_imag = total_imag + part_imag
    return jnp.stack([total_real, total_imag]).reshape(2, PROBES, PANELS)


def recip_apply(rounded, grid_row, grid_col, stencil, recip_kernel):
    weights = stencil.astype(jnp.float32)
    offsets = jnp.arange(STENCIL, dtype=jnp.int32)
    rows = (grid_row[None, None, :] + offsets[:, None, None]) % NG1
    cols = (grid_col[None, None, :] + offsets[None, :, None]) % NG2
    cells = rows * NG2 + cols
    values = weights[None, None, :, :, :] * rounded[:, :, None, None, :]
    grid = jnp.zeros((2, PROBES, NG1 * NG2), jnp.float32).at[:, :, cells].add(values)
    complex_grid = lax.complex(grid[0], grid[1]).reshape(PROBES, NG1, NG2)
    spectrum = jnp.fft.fft2(complex_grid) * recip_kernel
    field = jnp.fft.ifft2(spectrum).reshape(PROBES, NG1 * NG2)
    planes = jnp.stack([jnp.real(field), jnp.imag(field)]).astype(jnp.float32)
    planes = lax.optimization_barrier(planes.astype(jnp.bfloat16)).astype(jnp.float32)
    return jnp.sum(weights[None, None, :, :, :] * planes[:, :, cells], axis=(2, 3))


def apply_operator(source, near_blocks, bloch_angle, grid_row, grid_col, stencil, recip_kernel):
    rounded = lax.optimization_barrier(source.astype(jnp.bfloat16)).astype(jnp.float32)
    near_part = near_apply(rounded, near_blocks, bloch_angle)
    recip_part = recip_apply(rounded, grid_row, grid_col, stencil, recip_kernel)
    return 0.5 * source + near_part + recip_part


def reference(source_probes, near_blocks, bloch_angle, grid_row, grid_col, stencil, recip_kernel):
    first_image = apply_operator(source_probes, near_blocks, bloch_angle, grid_row, grid_col, stencil, recip_kernel)
    second_image = apply_operator(first_image, near_blocks, bloch_angle, grid_row, grid_col, stencil, recip_kernel)
    return first_image, second_image
```

```python
import math

import jax
import jax.numpy as jnp
from jax import lax
from jax.sharding import PartitionSpec as P

STENCIL = 4
NG1 = 512
NG2 = 512


HIGHEST = lax.Precision.HIGHEST
HIGH = lax.Precision.HIGH


def with_halo(cells, sides, width):
    for axis, dim in sides:
        count = lax.axis_size(axis)
        head = lax.slice_in_dim(cells, 0, width, axis=dim)
        tail = lax.slice_in_dim(cells, cells.shape[dim] - width, cells.shape[dim], axis=dim)
        cells = jnp.concatenate(
            [
                lax.ppermute(tail, axis, [(i, (i + 1) % count) for i in range(count)]),
                cells,
                lax.ppermute(head, axis, [((i + 1) % count, i) for i in range(count)]),
            ],
            axis=dim,
        )
    return cells


def shifted(array, axis, by):
    count = lax.axis_size(axis)
    return lax.ppermute(array, axis, [(i, (i + by) % count) for i in range(count)])


def twiddle(first_index, second_index, length):
    product = first_index[:, None] * second_index[None, :] % length
    phase_angle = 2.0 * math.pi / length * product.astype(jnp.float32)
    return (jnp.cos(phase_angle), jnp.sin(phase_angle))


def spread_matrix(grid_row, grid_col, stencil, rows_dev):
    panels = grid_row.shape[0]
    span = (rows_dev + STENCIL - 1) * NG2
    local_row = grid_row % rows_dev
    cells = lax.broadcasted_iota(jnp.int32, (panels, span), 1)
    matrix = jnp.zeros((panels, span), jnp.float32)
    for row_off in range(STENCIL):
        for col_off in range(STENCIL):
            target = (local_row + row_off) * NG2 + (grid_col + col_off) % NG2
            matrix = matrix + jnp.where(
                cells == target[:, None],
                stencil[row_off, col_off].astype(jnp.float32)[:, None],
                0.0,
            )
    return matrix.astype(jnp.bfloat16)


def near_term(rounded, near_blocks, bloch_angle):
    probe_rows = rounded.shape[1]
    panels = rounded.shape[2]
    packed = rounded.reshape(2 * probe_rows, 1, 1, panels)
    widened = with_halo(packed, (("tile", 1), ("sect", 2)), 1)
    tile_pos = lax.axis_index("tile")
    tile_count = lax.axis_size("tile")
    sect_pos = lax.axis_index("sect")
    sect_count = lax.axis_size("sect")
    total_real = jnp.zeros((probe_rows, panels), jnp.float32)
    total_imag = jnp.zeros((probe_rows, panels), jnp.float32)
    for tile_off in (-1, 0, 1):
        for sect_off in (-1, 0, 1):
            index = (tile_off + 1) * 3 + sect_off + 1
            piece = widened[:, tile_off + 1, sect_off + 1, :]
            with_real = jnp.dot(piece, near_blocks[0, index], preferred_element_type=jnp.float32)
            with_imag = jnp.dot(piece, near_blocks[1, index], preferred_element_type=jnp.float32)
            part_real = with_real[:probe_rows] - with_imag[probe_rows:]
            part_imag = with_real[probe_rows:] + with_imag[:probe_rows]
            if tile_off != 0 or sect_off != 0:
                phase_angle = jnp.float32(0.0)
                if tile_off != 0:
                    border = tile_pos == (tile_count - 1 if tile_off == 1 else 0)
                    phase_angle = jnp.where(border, bloch_angle[0] * tile_off, 0.0)
                if sect_off != 0:
                    border = sect_pos == (sect_count - 1 if sect_off == 1 else 0)
                    phase_angle = phase_angle + jnp.where(border, bloch_angle[1] * sect_off, 0.0)
                cos_part = jnp.cos(phase_angle)
                sin_part = jnp.sin(phase_angle)
                part_real, part_imag = (
                    part_real * cos_part - part_imag * sin_part,
                    part_real * sin_part + part_imag * cos_part,
                )
            total_real = total_real + part_real
            total_imag = total_imag + part_imag
    return jnp.stack([total_real, total_imag])


def recip_term(rounded, matrix, recip_kernel, col_table, row_forward, row_inverse):
    probe_rows = rounded.shape[1]
    extended = matrix.shape[1] // NG2
    rows_dev = extended - (STENCIL - 1)
    flat = rounded.reshape(2 * probe_rows, rounded.shape[2])
    spread = jnp.dot(flat, matrix, preferred_element_type=jnp.float32)
    spread = spread.reshape(2 * probe_rows, extended, NG2)
    overflow = spread[:, rows_dev:]
    incoming = shifted(overflow, ("tile", "sect"), 1)
    grid = jnp.concatenate(
        [spread[:, : STENCIL - 1] + incoming, spread[:, STENCIL - 1 : rows_dev]], axis=1
    )
    grid = grid.transpose(1, 0, 2).reshape(rows_dev * 2 * probe_rows, NG2)
    mixed = jnp.dot(grid, col_table, precision=HIGHEST, preferred_element_type=jnp.float32)
    mixed = mixed.reshape(rows_dev, 2, probe_rows, 2, NG2)
    spec_real = mixed[:, 0, :, 0] + mixed[:, 1, :, 1]
    spec_imag = mixed[:, 1, :, 0] - mixed[:, 0, :, 1]
    spectrum = jnp.stack([spec_real, spec_imag], axis=1).reshape(rows_dev, 2 * probe_rows, NG2)
    columns = lax.all_to_all(spectrum, ("tile", "sect"), split_axis=2, concat_axis=0, tiled=True)
    cols_dev = columns.shape[2]
    stacked = jnp.dot(
        row_forward,
        columns.reshape(NG1, 2 * probe_rows * cols_dev),
        precision=HIGHEST,
        preferred_element_type=jnp.float32,
    )
    stacked = stacked.reshape(2, NG1, 2, probe_rows, cols_dev)
    scale = recip_kernel[:, None, :] / (NG1 * NG2)
    freq_real = (stacked[0, :, 0] + stacked[1, :, 1]) * scale
    freq_imag = (stacked[0, :, 1] - stacked[1, :, 0]) * scale
    freq = jnp.stack([freq_real, freq_imag], axis=1).reshape(NG1, 2 * probe_rows * cols_dev)
    back = jnp.dot(row_inverse, freq, precision=HIGHEST, preferred_element_type=jnp.float32)
    back = back.reshape(2, NG1, 2, probe_rows, cols_dev)
    out_real = back[0, :, 0] - back[1, :, 1]
    out_imag = back[0, :, 1] + back[1, :, 0]
    spatial = jnp.stack([out_real, out_imag], axis=1).reshape(NG1, 2 * probe_rows, cols_dev)
    row_blocks = lax.all_to_all(spatial, ("tile", "sect"), split_axis=0, concat_axis=2, tiled=True)
    mixed = jnp.dot(
        row_blocks.reshape(rows_dev * 2 * probe_rows, NG2),
        col_table,
        precision=HIGHEST,
        preferred_element_type=jnp.float32,
    )
    mixed = mixed.reshape(rows_dev, 2, probe_rows, 2, NG2)
    field_real = mixed[:, 0, :, 0] - mixed[:, 1, :, 1]
    field_imag = mixed[:, 1, :, 0] + mixed[:, 0, :, 1]
    field = (
        jnp.stack([field_real, field_imag], axis=0)
        .transpose(0, 2, 1, 3)
        .reshape(2 * probe_rows, rows_dev, NG2)
    )
    field_low = field.astype(jnp.bfloat16)
    following = shifted(field_low[:, : STENCIL - 1], ("tile", "sect"), -1)
    whole = jnp.concatenate([field_low, following], axis=1).reshape(2 * probe_rows, extended * NG2)
    result = lax.dot_general(
        whole, matrix, (((1,), (1,)), ((), ())), preferred_element_type=jnp.float32
    )
    return result.reshape(2, probe_rows, rounded.shape[2])


def local_by_column(source_probes, near_blocks, bloch_angle, grid_row, grid_col, stencil, recip_kernel):
    tile_count = lax.axis_size("tile")
    sect_count = lax.axis_size("sect")
    rows_dev = NG1 // (tile_count * sect_count)
    matrix = spread_matrix(grid_row, grid_col, stencil, rows_dev)
    col_index = jnp.arange(NG2, dtype=jnp.int32)
    col_cos, col_sin = twiddle(col_index, col_index, NG2)
    col_table = jnp.concatenate([col_cos, col_sin], axis=1)
    position = jnp.arange(NG1, dtype=jnp.int32)
    forward_cos, forward_sin = twiddle(position, position, NG1)
    row_forward = jnp.concatenate([forward_cos, forward_sin], axis=0)
    inverse_cos, inverse_sin = twiddle(position, position, NG1)
    row_inverse = jnp.concatenate([inverse_cos, inverse_sin], axis=0)

    def apply_operator(source):
        rounded = source.astype(jnp.bfloat16)
        near_part = near_term(rounded, near_blocks, bloch_angle)
        recip_part = recip_term(rounded, matrix, recip_kernel, col_table, row_forward, row_inverse)
        return 0.5 * source + near_part + recip_part

    first_image = apply_operator(source_probes)
    second_image = apply_operator(first_image)
    return (first_image, second_image)


def probe_tables(grid_row, grid_col, stencil, recip_kernel, rows_dev, extended):
    axes = ("tile", "sect")
    panels = grid_row.shape[0]
    taps = STENCIL * STENCIL
    packed = jnp.concatenate(
        [
            stencil.reshape(taps, panels),
            (grid_row % rows_dev).astype(jnp.bfloat16)[None],
            (grid_col // 256).astype(jnp.bfloat16)[None],
            (grid_col % 256).astype(jnp.bfloat16)[None],
        ],
        axis=0,
    )
    packed = lax.all_gather(packed, axes, axis=0)
    local_row = packed[:, taps].astype(jnp.int32)
    column = packed[:, taps + 1].astype(jnp.int32) * 256 + packed[:, taps + 2].astype(jnp.int32)
    weights = packed[:, :taps].reshape(-1, STENCIL, STENCIL, panels)
    blocks = packed.shape[0]
    cells = lax.broadcasted_iota(jnp.int32, (1, NG2, 1, 1), 1)
    delta = cells - column[:, None, None, :]
    delta = jnp.where(delta < 0, delta + NG2, delta)
    cols = jnp.zeros((blocks, NG2, STENCIL, panels), jnp.bfloat16)
    for col_off in range(STENCIL):
        cols = jnp.where(delta == col_off, weights[:, None, :, col_off], cols)
    cols = cols.reshape(blocks, NG2, STENCIL * panels)
    kernel = lax.all_gather(recip_kernel.T / (NG1 * NG2), axes, axis=0, tiled=True).T
    return local_row, cols, kernel


def row_table(blocks, rows_dev, extended):
    shape = (2, NG1, blocks, 2, extended)
    out_part = lax.broadcasted_iota(jnp.int32, shape, 0)
    freq = lax.broadcasted_iota(jnp.int32, shape, 1)
    block = lax.broadcasted_iota(jnp.int32, shape, 2)
    in_part = lax.broadcasted_iota(jnp.int32, shape, 3)
    row = lax.broadcasted_iota(jnp.int32, shape, 4)
    turn = freq * (block * rows_dev + row) % NG1
    turn = (turn + (out_part - in_part) * (NG1 // 4) + NG1) % NG1
    table = jnp.cos(2.0 * math.pi / NG1 * turn.astype(jnp.float32))
    table = jnp.where(row < rows_dev + STENCIL - 1, table, 0.0)
    return table.reshape(2 * NG1, blocks * 2 * extended)


def probe_recip(rounded, local_row, cols, kernel, rows, col_table, extended):
    axes = ("tile", "sect")
    probes, panels = rounded.shape[1], rounded.shape[2]
    blocks = local_row.shape[0]
    held = probes // blocks
    mine = lax.all_to_all(rounded.transpose(1, 0, 2), axes, split_axis=0, concat_axis=0, tiled=True)
    mine = mine.reshape(blocks, held, 2, panels)
    tap_row = local_row[:, None, :] + lax.broadcasted_iota(jnp.int32, (1, STENCIL, 1), 1)
    place = lax.broadcasted_iota(jnp.int32, (1, extended, 1, 1), 1)
    hit = tap_row[:, None] == place
    results = []
    for q in range(held):
        spread = jnp.where(hit[:, None], mine[:, q, :, None, None, :], 0)
        spread = spread.reshape(blocks, 2 * extended, STENCIL * panels)
        grid = lax.dot_general(
            spread, cols, (((2,), (2,)), ((0,), (0,))), preferred_element_type=jnp.float32
        ).reshape(blocks * 2 * extended, NG2)
        freq = jnp.dot(rows, grid, precision=HIGH, preferred_element_type=jnp.float32)
        freq = jnp.dot(freq, col_table, precision=HIGH, preferred_element_type=jnp.float32)
        freq_real = (freq[:NG1, :NG2] + freq[NG1:, NG2:]) * kernel
        freq_imag = (freq[NG1:, :NG2] - freq[:NG1, NG2:]) * kernel
        freq = jnp.concatenate([freq_real, freq_imag], axis=0)
        back = jnp.dot(freq, col_table, precision=HIGH, preferred_element_type=jnp.float32)
        back_real = back[:NG1, :NG2] - back[NG1:, NG2:]
        back_imag = back[NG1:, :NG2] + back[:NG1, NG2:]
        back = jnp.concatenate([back_real, back_imag], axis=0)
        field = lax.dot_general(
            rows, back, (((0,), (0,)), ((), ())), precision=HIGH, preferred_element_type=jnp.float32
        )
        field = field.astype(jnp.bfloat16).reshape(blocks, 2 * extended, NG2)
        taken = lax.dot_general(
            field, cols, (((2,), (1,)), ((0,), (0,))), preferred_element_type=jnp.float32
        ).reshape(blocks, 2, extended, STENCIL, panels)
        results.append(jnp.sum(jnp.where(hit[:, None], taken, 0.0), axis=(2, 3)))
    result = jnp.stack(results, axis=1).reshape(probes, 2, panels)
    result = lax.all_to_all(result, axes, split_axis=0, concat_axis=0, tiled=True)
    return result.transpose(1, 0, 2)


def local_by_probe(
    source_probes, near_blocks, bloch_angle, grid_row, grid_col, stencil, recip_kernel
):
    blocks = lax.axis_size("tile") * lax.axis_size("sect")
    rows_dev = NG1 // blocks
    extended = -(-(rows_dev + STENCIL - 1) // 8) * 8
    local_row, cols, kernel = probe_tables(
        grid_row, grid_col, stencil, recip_kernel, rows_dev, extended
    )
    rows = row_table(blocks, rows_dev, extended)
    col_index = jnp.arange(NG2, dtype=jnp.int32)
    col_table = jnp.concatenate(twiddle(col_index, col_index, NG2), axis=1)

    def apply_operator(source):
        rounded = source.astype(jnp.bfloat16)
        near_part = near_term(rounded, near_blocks, bloch_angle)
        recip_part = probe_recip(rounded, local_row, cols, kernel, rows, col_table, extended)
        return 0.5 * source + near_part + recip_part

    first_image = apply_operator(source_probes)
    second_image = apply_operator(first_image)
    return (first_image, second_image)


def local(source_probes, *rest):
    blocks = lax.axis_size("tile") * lax.axis_size("sect")
    if source_probes.shape[1] % blocks == 0:
        return local_by_probe(source_probes, *rest)
    return local_by_column(source_probes, *rest)


def solution(mesh):
    return jax.shard_map(
        local,
        mesh=mesh,
        in_specs=(
            P(None, "groups", ("tile", "sect")),
            P("groups", None, None, ("tile", "sect")),
            P("groups"),
            P(("tile", "sect")),
            P(("tile", "sect")),
            P(None, None, ("tile", "sect")),
            P("groups", ("tile", "sect")),
        ),
        out_specs=(P(None, "groups", ("tile", "sect")), P(None, "groups", ("tile", "sect"))),
        check_vma=False,
    )
```

```python
import math

import jax
import jax.numpy as jnp
from jax import lax
from jax.experimental import pallas as pl
from jax.experimental.pallas import tpu as pltpu
from jax.sharding import PartitionSpec as P

STENCIL = 4
NG1 = 512
NG2 = 512


HIGHEST = lax.Precision.HIGHEST
HIGH = lax.Precision.HIGH


def with_halo(cells, sides, width):
    for axis, dim in sides:
        count = lax.axis_size(axis)
        head = lax.slice_in_dim(cells, 0, width, axis=dim)
        tail = lax.slice_in_dim(cells, cells.shape[dim] - width, cells.shape[dim], axis=dim)
        cells = jnp.concatenate(
            [
                lax.ppermute(tail, axis, [(i, (i + 1) % count) for i in range(count)]),
                cells,
                lax.ppermute(head, axis, [((i + 1) % count, i) for i in range(count)]),
            ],
            axis=dim,
        )
    return cells


def shifted(array, axis, by):
    count = lax.axis_size(axis)
    return lax.ppermute(array, axis, [(i, (i + by) % count) for i in range(count)])


def twiddle(first_index, second_index, length):
    product = first_index[:, None] * second_index[None, :] % length
    phase_angle = 2.0 * math.pi / length * product.astype(jnp.float32)
    return (jnp.cos(phase_angle), jnp.sin(phase_angle))


def spread_matrix(grid_row, grid_col, stencil, rows_dev):
    panels = grid_row.shape[0]
    span = (rows_dev + STENCIL - 1) * NG2
    local_row = grid_row % rows_dev
    cells = lax.broadcasted_iota(jnp.int32, (panels, span), 1)
    matrix = jnp.zeros((panels, span), jnp.float32)
    for row_off in range(STENCIL):
        for col_off in range(STENCIL):
            target = (local_row + row_off) * NG2 + (grid_col + col_off) % NG2
            matrix = matrix + jnp.where(
                cells == target[:, None],
                stencil[row_off, col_off].astype(jnp.float32)[:, None],
                0.0,
            )
    return matrix.astype(jnp.bfloat16)


def near_term(rounded, near_blocks, bloch_angle):
    probe_rows = rounded.shape[1]
    panels = rounded.shape[2]
    packed = rounded.reshape(2 * probe_rows, 1, 1, panels)
    widened = with_halo(packed, (("tile", 1), ("sect", 2)), 1)
    tile_pos = lax.axis_index("tile")
    tile_count = lax.axis_size("tile")
    sect_pos = lax.axis_index("sect")
    sect_count = lax.axis_size("sect")
    total_real = jnp.zeros((probe_rows, panels), jnp.float32)
    total_imag = jnp.zeros((probe_rows, panels), jnp.float32)
    for tile_off in (-1, 0, 1):
        for sect_off in (-1, 0, 1):
            index = (tile_off + 1) * 3 + sect_off + 1
            piece = widened[:, tile_off + 1, sect_off + 1, :]
            with_real = jnp.dot(piece, near_blocks[0, index], preferred_element_type=jnp.float32)
            with_imag = jnp.dot(piece, near_blocks[1, index], preferred_element_type=jnp.float32)
            part_real = with_real[:probe_rows] - with_imag[probe_rows:]
            part_imag = with_real[probe_rows:] + with_imag[:probe_rows]
            if tile_off != 0 or sect_off != 0:
                phase_angle = jnp.float32(0.0)
                if tile_off != 0:
                    border = tile_pos == (tile_count - 1 if tile_off == 1 else 0)
                    phase_angle = jnp.where(border, bloch_angle[0] * tile_off, 0.0)
                if sect_off != 0:
                    border = sect_pos == (sect_count - 1 if sect_off == 1 else 0)
                    phase_angle = phase_angle + jnp.where(border, bloch_angle[1] * sect_off, 0.0)
                cos_part = jnp.cos(phase_angle)
                sin_part = jnp.sin(phase_angle)
                part_real, part_imag = (
                    part_real * cos_part - part_imag * sin_part,
                    part_real * sin_part + part_imag * cos_part,
                )
            total_real = total_real + part_real
            total_imag = total_imag + part_imag
    return jnp.stack([total_real, total_imag])


def recip_term(rounded, matrix, recip_kernel, col_table, row_forward, row_inverse):
    probe_rows = rounded.shape[1]
    extended = matrix.shape[1] // NG2
    rows_dev = extended - (STENCIL - 1)
    flat = rounded.reshape(2 * probe_rows, rounded.shape[2])
    spread = jnp.dot(flat, matrix, preferred_element_type=jnp.float32)
    spread = spread.reshape(2 * probe_rows, extended, NG2)
    overflow = spread[:, rows_dev:]
    incoming = shifted(overflow, ("tile", "sect"), 1)
    grid = jnp.concatenate(
        [spread[:, : STENCIL - 1] + incoming, spread[:, STENCIL - 1 : rows_dev]], axis=1
    )
    grid = grid.transpose(1, 0, 2).reshape(rows_dev * 2 * probe_rows, NG2)
    mixed = jnp.dot(grid, col_table, precision=HIGHEST, preferred_element_type=jnp.float32)
    mixed = mixed.reshape(rows_dev, 2, probe_rows, 2, NG2)
    spec_real = mixed[:, 0, :, 0] + mixed[:, 1, :, 1]
    spec_imag = mixed[:, 1, :, 0] - mixed[:, 0, :, 1]
    spectrum = jnp.stack([spec_real, spec_imag], axis=1).reshape(rows_dev, 2 * probe_rows, NG2)
    columns = lax.all_to_all(spectrum, ("tile", "sect"), split_axis=2, concat_axis=0, tiled=True)
    cols_dev = columns.shape[2]
    stacked = jnp.dot(
        row_forward,
        columns.reshape(NG1, 2 * probe_rows * cols_dev),
        precision=HIGHEST,
        preferred_element_type=jnp.float32,
    )
    stacked = stacked.reshape(2, NG1, 2, probe_rows, cols_dev)
    scale = recip_kernel[:, None, :] / (NG1 * NG2)
    freq_real = (stacked[0, :, 0] + stacked[1, :, 1]) * scale
    freq_imag = (stacked[0, :, 1] - stacked[1, :, 0]) * scale
    freq = jnp.stack([freq_real, freq_imag], axis=1).reshape(NG1, 2 * probe_rows * cols_dev)
    back = jnp.dot(row_inverse, freq, precision=HIGHEST, preferred_element_type=jnp.float32)
    back = back.reshape(2, NG1, 2, probe_rows, cols_dev)
    out_real = back[0, :, 0] - back[1, :, 1]
    out_imag = back[0, :, 1] + back[1, :, 0]
    spatial = jnp.stack([out_real, out_imag], axis=1).reshape(NG1, 2 * probe_rows, cols_dev)
    row_blocks = lax.all_to_all(spatial, ("tile", "sect"), split_axis=0, concat_axis=2, tiled=True)
    mixed = jnp.dot(
        row_blocks.reshape(rows_dev * 2 * probe_rows, NG2),
        col_table,
        precision=HIGHEST,
        preferred_element_type=jnp.float32,
    )
    mixed = mixed.reshape(rows_dev, 2, probe_rows, 2, NG2)
    field_real = mixed[:, 0, :, 0] - mixed[:, 1, :, 1]
    field_imag = mixed[:, 1, :, 0] + mixed[:, 0, :, 1]
    field = (
        jnp.stack([field_real, field_imag], axis=0)
        .transpose(0, 2, 1, 3)
        .reshape(2 * probe_rows, rows_dev, NG2)
    )
    field_low = field.astype(jnp.bfloat16)
    following = shifted(field_low[:, : STENCIL - 1], ("tile", "sect"), -1)
    whole = jnp.concatenate([field_low, following], axis=1).reshape(2 * probe_rows, extended * NG2)
    result = lax.dot_general(
        whole, matrix, (((1,), (1,)), ((), ())), preferred_element_type=jnp.float32
    )
    return result.reshape(2, probe_rows, rounded.shape[2])


def local_by_column(source_probes, near_blocks, bloch_angle, grid_row, grid_col, stencil, recip_kernel):
    tile_count = lax.axis_size("tile")
    sect_count = lax.axis_size("sect")
    rows_dev = NG1 // (tile_count * sect_count)
    matrix = spread_matrix(grid_row, grid_col, stencil, rows_dev)
    col_index = jnp.arange(NG2, dtype=jnp.int32)
    col_cos, col_sin = twiddle(col_index, col_index, NG2)
    col_table = jnp.concatenate([col_cos, col_sin], axis=1)
    position = jnp.arange(NG1, dtype=jnp.int32)
    forward_cos, forward_sin = twiddle(position, position, NG1)
    row_forward = jnp.concatenate([forward_cos, forward_sin], axis=0)
    inverse_cos, inverse_sin = twiddle(position, position, NG1)
    row_inverse = jnp.concatenate([inverse_cos, inverse_sin], axis=0)

    def apply_operator(source):
        rounded = source.astype(jnp.bfloat16)
        near_part = near_term(rounded, near_blocks, bloch_angle)
        recip_part = recip_term(rounded, matrix, recip_kernel, col_table, row_forward, row_inverse)
        return 0.5 * source + near_part + recip_part

    first_image = apply_operator(source_probes)
    second_image = apply_operator(first_image)
    return (first_image, second_image)


def cols_kernel(column_ref, weights_ref, cols_ref):
    panels = column_ref.shape[-1]
    chunk = 16

    def step(index, carry):
        start = pl.multiple_of(index * chunk, chunk)
        cells = lax.broadcasted_iota(jnp.int32, (chunk, panels), 0) + start
        delta = cells - column_ref[0]
        delta = jnp.where(delta < 0, delta + NG2, delta)
        for row_off in range(STENCIL):
            values = jnp.zeros((chunk, panels), jnp.float32)
            for col_off in range(STENCIL):
                tap = row_off * STENCIL + col_off
                values = jnp.where(delta == col_off, weights_ref[0, tap : tap + 1], values)
            cols_ref[0, pl.ds(start, chunk), row_off * panels : (row_off + 1) * panels] = (
                values.astype(jnp.bfloat16)
            )
        return carry

    lax.fori_loop(0, NG2 // chunk, step, 0)


def build_cols(column, weights):
    blocks, _, panels = column.shape
    return pl.pallas_call(
        cols_kernel,
        grid=(blocks,),
        in_specs=[
            pl.BlockSpec((1, 1, panels), lambda b: (b, 0, 0)),
            pl.BlockSpec((1, STENCIL * STENCIL, panels), lambda b: (b, 0, 0)),
        ],
        out_specs=pl.BlockSpec((1, NG2, STENCIL * panels), lambda b: (b, 0, 0)),
        out_shape=jax.ShapeDtypeStruct((blocks, NG2, STENCIL * panels), jnp.bfloat16),
        compiler_params=pltpu.CompilerParams(vmem_limit_bytes=24 << 20),
    )(column, weights)


def spread_kernel(values_ref, row_ref, cols_ref, grid_ref, left_ref):
    extended = grid_ref.shape[2]
    panels = row_ref.shape[-1]
    place = lax.broadcasted_iota(jnp.int32, (extended, panels), 0)
    for row_off in range(STENCIL):
        hit = place == row_ref[0] + row_off
        parts = [jnp.where(hit, values_ref[0, c : c + 1], 0.0) for c in range(2)]
        left_ref[:, row_off * panels : (row_off + 1) * panels] = jnp.concatenate(
            parts, axis=0
        ).astype(jnp.bfloat16)
    grid = lax.dot_general(
        left_ref[...], cols_ref[0], (((1,), (1,)), ((), ())), preferred_element_type=jnp.float32
    )
    grid_ref[...] = grid.reshape(grid_ref.shape)


def spread(values, local_row, cols, extended):
    blocks, _, panels = local_row.shape
    return pl.pallas_call(
        spread_kernel,
        grid=(blocks,),
        in_specs=[
            pl.BlockSpec((1, 2, panels), lambda b: (b, 0, 0)),
            pl.BlockSpec((1, 1, panels), lambda b: (b, 0, 0)),
            pl.BlockSpec((1, NG2, STENCIL * panels), lambda b: (b, 0, 0)),
        ],
        out_specs=pl.BlockSpec((2, 1, extended, NG2), lambda b: (0, b, 0, 0)),
        out_shape=jax.ShapeDtypeStruct((2, blocks, extended, NG2), jnp.float32),
        scratch_shapes=[pltpu.VMEM((2 * extended, STENCIL * panels), jnp.bfloat16)],
        compiler_params=pltpu.CompilerParams(vmem_limit_bytes=24 << 20),
    )(values, local_row, cols)


def take_kernel(field_ref, row_ref, cols_ref, out_ref):
    extended = field_ref.shape[2]
    panels = row_ref.shape[-1]
    field = field_ref[...].reshape(2 * extended, NG2).astype(jnp.bfloat16)
    place = lax.broadcasted_iota(jnp.int32, (extended, panels), 0)
    place = jnp.concatenate([place, place], axis=0)
    total = jnp.zeros((2 * extended, panels), jnp.float32)
    for row_off in range(STENCIL):
        taken = jnp.dot(
            field,
            cols_ref[0, :, row_off * panels : (row_off + 1) * panels],
            preferred_element_type=jnp.float32,
        )
        total = total + jnp.where(place == row_ref[0] + row_off, taken, 0.0)
    out_ref[0] = jnp.sum(total.reshape(2, extended, panels), axis=1)


def take(field, local_row, cols):
    _, blocks, extended, _ = field.shape
    panels = local_row.shape[-1]
    return pl.pallas_call(
        take_kernel,
        grid=(blocks,),
        in_specs=[
            pl.BlockSpec((2, 1, extended, NG2), lambda b: (0, b, 0, 0)),
            pl.BlockSpec((1, 1, panels), lambda b: (b, 0, 0)),
            pl.BlockSpec((1, NG2, STENCIL * panels), lambda b: (b, 0, 0)),
        ],
        out_specs=pl.BlockSpec((1, 2, panels), lambda b: (b, 0, 0)),
        out_shape=jax.ShapeDtypeStruct((blocks, 2, panels), jnp.float32),
        compiler_params=pltpu.CompilerParams(vmem_limit_bytes=24 << 20),
    )(field, local_row, cols)


def probe_tables(grid_row, grid_col, stencil, recip_kernel, rows_dev):
    axes = ("tile", "sect")
    blocks = lax.axis_size("tile") * lax.axis_size("sect")
    panels = grid_row.shape[0]
    taps = STENCIL * STENCIL
    packed = jnp.concatenate(
        [
            stencil.reshape(taps, panels),
            (grid_row % rows_dev).astype(jnp.bfloat16)[None],
            (grid_col // 256).astype(jnp.bfloat16)[None],
            (grid_col % 256).astype(jnp.bfloat16)[None],
        ],
        axis=0,
    )
    packed = jnp.broadcast_to(packed[None], (blocks,) + packed.shape)
    packed = lax.all_to_all(packed, axes, split_axis=0, concat_axis=0, tiled=True)
    packed = packed.astype(jnp.float32)
    local_row = packed[:, taps : taps + 1].astype(jnp.int32)
    column = packed[:, taps + 1 : taps + 2] * 256 + packed[:, taps + 2 :]
    cols = build_cols(column.astype(jnp.int32), packed[:, :taps])
    kernel = lax.all_gather(recip_kernel.T / (NG1 * NG2), axes, axis=0, tiled=True).T
    return local_row, cols, kernel


def row_table(blocks, rows_dev, extended):
    place = jnp.arange(blocks * extended, dtype=jnp.int32)
    row = place % extended
    grid_row = place // extended * rows_dev + row
    used = (row < rows_dev + STENCIL - 1)[None, :]
    cos, sin = twiddle(jnp.arange(NG1, dtype=jnp.int32), grid_row, NG1)
    cos, sin = jnp.where(used, cos, 0.0), jnp.where(used, sin, 0.0)
    return jnp.concatenate(
        [jnp.concatenate([cos, sin], axis=1), jnp.concatenate([-sin, cos], axis=1)], axis=0
    )


def probe_recip(rounded, local_row, cols, kernel, rows, col_table, extended):
    axes = ("tile", "sect")
    probes, panels = rounded.shape[1], rounded.shape[2]
    blocks = local_row.shape[0]
    held = probes // blocks
    mine = lax.all_to_all(rounded.transpose(1, 0, 2), axes, split_axis=0, concat_axis=0, tiled=True)
    mine = mine.reshape(blocks, held, 2, panels).astype(jnp.float32)
    results = []
    for q in range(held):
        grid = spread(mine[:, q], local_row, cols, extended).reshape(-1, NG2)
        freq = jnp.dot(rows, grid, precision=HIGH, preferred_element_type=jnp.float32)
        freq = jnp.dot(freq, col_table, precision=HIGH, preferred_element_type=jnp.float32)
        freq_real = (freq[:NG1, :NG2] + freq[NG1:, NG2:]) * kernel
        freq_imag = (freq[NG1:, :NG2] - freq[:NG1, NG2:]) * kernel
        freq = jnp.concatenate([freq_real, freq_imag], axis=0)
        back = jnp.dot(freq, col_table, precision=HIGH, preferred_element_type=jnp.float32)
        back_real = back[:NG1, :NG2] - back[NG1:, NG2:]
        back_imag = back[NG1:, :NG2] + back[:NG1, NG2:]
        back = jnp.concatenate([back_real, back_imag], axis=0)
        field = lax.dot_general(
            rows, back, (((0,), (0,)), ((), ())), precision=HIGH, preferred_element_type=jnp.float32
        )
        results.append(take(field.reshape(2, blocks, extended, NG2), local_row, cols))
    result = jnp.stack(results, axis=1).reshape(probes, 2, panels)
    result = lax.all_to_all(result, axes, split_axis=0, concat_axis=0, tiled=True)
    return result.transpose(1, 0, 2)


def local_by_probe(
    source_probes, near_blocks, bloch_angle, grid_row, grid_col, stencil, recip_kernel
):
    blocks = lax.axis_size("tile") * lax.axis_size("sect")
    rows_dev = NG1 // blocks
    extended = -(-(rows_dev + STENCIL - 1) // 8) * 8
    local_row, cols, kernel = probe_tables(grid_row, grid_col, stencil, recip_kernel, rows_dev)
    rows = row_table(blocks, rows_dev, extended)
    col_index = jnp.arange(NG2, dtype=jnp.int32)
    col_table = jnp.concatenate(twiddle(col_index, col_index, NG2), axis=1)
    rows, col_table = lax.optimization_barrier((rows, col_table))

    def apply_operator(source):
        rounded = source.astype(jnp.bfloat16)
        near_part = near_term(rounded, near_blocks, bloch_angle)
        recip_part = probe_recip(rounded, local_row, cols, kernel, rows, col_table, extended)
        return 0.5 * source + near_part + recip_part

    first_image = apply_operator(source_probes)
    second_image = apply_operator(first_image)
    return (first_image, second_image)


def local(source_probes, *rest):
    blocks = lax.axis_size("tile") * lax.axis_size("sect")
    if source_probes.shape[1] % blocks == 0:
        return local_by_probe(source_probes, *rest)
    return local_by_column(source_probes, *rest)


def solution(mesh):
    return jax.shard_map(
        local,
        mesh=mesh,
        in_specs=(
            P(None, "groups", ("tile", "sect")),
            P("groups", None, None, ("tile", "sect")),
            P("groups"),
            P(("tile", "sect")),
            P(("tile", "sect")),
            P(None, None, ("tile", "sect")),
            P("groups", ("tile", "sect")),
        ),
        out_specs=(P(None, "groups", ("tile", "sect")), P(None, "groups", ("tile", "sect"))),
        check_vma=False,
    )
```

```python
import math

import jax
import jax.numpy as jnp
from jax import lax
from jax.experimental import pallas as pl
from jax.experimental.pallas import tpu as pltpu
from jax.sharding import PartitionSpec as P

STENCIL = 4
NG1 = 512
NG2 = 512


HIGHEST = lax.Precision.HIGHEST
HIGH = lax.Precision.HIGH


def with_halo(cells, sides, width):
    for axis, dim in sides:
        count = lax.axis_size(axis)
        head = lax.slice_in_dim(cells, 0, width, axis=dim)
        tail = lax.slice_in_dim(cells, cells.shape[dim] - width, cells.shape[dim], axis=dim)
        cells = jnp.concatenate(
            [
                lax.ppermute(tail, axis, [(i, (i + 1) % count) for i in range(count)]),
                cells,
                lax.ppermute(head, axis, [((i + 1) % count, i) for i in range(count)]),
            ],
            axis=dim,
        )
    return cells


def shifted(array, axis, by):
    count = lax.axis_size(axis)
    return lax.ppermute(array, axis, [(i, (i + by) % count) for i in range(count)])


def twiddle(first_index, second_index, length):
    product = first_index[:, None] * second_index[None, :] % length
    phase_angle = 2.0 * math.pi / length * product.astype(jnp.float32)
    return (jnp.cos(phase_angle), jnp.sin(phase_angle))


def spread_matrix(grid_row, grid_col, stencil, rows_dev):
    panels = grid_row.shape[0]
    span = (rows_dev + STENCIL - 1) * NG2
    local_row = grid_row % rows_dev
    cells = lax.broadcasted_iota(jnp.int32, (panels, span), 1)
    matrix = jnp.zeros((panels, span), jnp.float32)
    for row_off in range(STENCIL):
        for col_off in range(STENCIL):
            target = (local_row + row_off) * NG2 + (grid_col + col_off) % NG2
            matrix = matrix + jnp.where(
                cells == target[:, None],
                stencil[row_off, col_off].astype(jnp.float32)[:, None],
                0.0,
            )
    return matrix.astype(jnp.bfloat16)


def near_term(rounded, near_blocks, bloch_angle):
    probe_rows = rounded.shape[1]
    panels = rounded.shape[2]
    packed = rounded.reshape(2 * probe_rows, 1, 1, panels)
    widened = with_halo(packed, (("tile", 1), ("sect", 2)), 1)
    tile_pos = lax.axis_index("tile")
    tile_count = lax.axis_size("tile")
    sect_pos = lax.axis_index("sect")
    sect_count = lax.axis_size("sect")
    total_real = jnp.zeros((probe_rows, panels), jnp.float32)
    total_imag = jnp.zeros((probe_rows, panels), jnp.float32)
    for tile_off in (-1, 0, 1):
        for sect_off in (-1, 0, 1):
            index = (tile_off + 1) * 3 + sect_off + 1
            piece = widened[:, tile_off + 1, sect_off + 1, :]
            with_real = jnp.dot(piece, near_blocks[0, index], preferred_element_type=jnp.float32)
            with_imag = jnp.dot(piece, near_blocks[1, index], preferred_element_type=jnp.float32)
            part_real = with_real[:probe_rows] - with_imag[probe_rows:]
            part_imag = with_real[probe_rows:] + with_imag[:probe_rows]
            if tile_off != 0 or sect_off != 0:
                phase_angle = jnp.float32(0.0)
                if tile_off != 0:
                    border = tile_pos == (tile_count - 1 if tile_off == 1 else 0)
                    phase_angle = jnp.where(border, bloch_angle[0] * tile_off, 0.0)
                if sect_off != 0:
                    border = sect_pos == (sect_count - 1 if sect_off == 1 else 0)
                    phase_angle = phase_angle + jnp.where(border, bloch_angle[1] * sect_off, 0.0)
                cos_part = jnp.cos(phase_angle)
                sin_part = jnp.sin(phase_angle)
                part_real, part_imag = (
                    part_real * cos_part - part_imag * sin_part,
                    part_real * sin_part + part_imag * cos_part,
                )
            total_real = total_real + part_real
            total_imag = total_imag + part_imag
    return jnp.stack([total_real, total_imag])


def recip_term(rounded, matrix, recip_kernel, col_table, row_forward, row_inverse):
    probe_rows = rounded.shape[1]
    extended = matrix.shape[1] // NG2
    rows_dev = extended - (STENCIL - 1)
    flat = rounded.reshape(2 * probe_rows, rounded.shape[2])
    spread = jnp.dot(flat, matrix, preferred_element_type=jnp.float32)
    spread = spread.reshape(2 * probe_rows, extended, NG2)
    overflow = spread[:, rows_dev:]
    incoming = shifted(overflow, ("tile", "sect"), 1)
    grid = jnp.concatenate(
        [spread[:, : STENCIL - 1] + incoming, spread[:, STENCIL - 1 : rows_dev]], axis=1
    )
    grid = grid.transpose(1, 0, 2).reshape(rows_dev * 2 * probe_rows, NG2)
    mixed = jnp.dot(grid, col_table, precision=HIGHEST, preferred_element_type=jnp.float32)
    mixed = mixed.reshape(rows_dev, 2, probe_rows, 2, NG2)
    spec_real = mixed[:, 0, :, 0] + mixed[:, 1, :, 1]
    spec_imag = mixed[:, 1, :, 0] - mixed[:, 0, :, 1]
    spectrum = jnp.stack([spec_real, spec_imag], axis=1).reshape(rows_dev, 2 * probe_rows, NG2)
    columns = lax.all_to_all(spectrum, ("tile", "sect"), split_axis=2, concat_axis=0, tiled=True)
    cols_dev = columns.shape[2]
    stacked = jnp.dot(
        row_forward,
        columns.reshape(NG1, 2 * probe_rows * cols_dev),
        precision=HIGHEST,
        preferred_element_type=jnp.float32,
    )
    stacked = stacked.reshape(2, NG1, 2, probe_rows, cols_dev)
    scale = recip_kernel[:, None, :] / (NG1 * NG2)
    freq_real = (stacked[0, :, 0] + stacked[1, :, 1]) * scale
    freq_imag = (stacked[0, :, 1] - stacked[1, :, 0]) * scale
    freq = jnp.stack([freq_real, freq_imag], axis=1).reshape(NG1, 2 * probe_rows * cols_dev)
    back = jnp.dot(row_inverse, freq, precision=HIGHEST, preferred_element_type=jnp.float32)
    back = back.reshape(2, NG1, 2, probe_rows, cols_dev)
    out_real = back[0, :, 0] - back[1, :, 1]
    out_imag = back[0, :, 1] + back[1, :, 0]
    spatial = jnp.stack([out_real, out_imag], axis=1).reshape(NG1, 2 * probe_rows, cols_dev)
    row_blocks = lax.all_to_all(spatial, ("tile", "sect"), split_axis=0, concat_axis=2, tiled=True)
    mixed = jnp.dot(
        row_blocks.reshape(rows_dev * 2 * probe_rows, NG2),
        col_table,
        precision=HIGHEST,
        preferred_element_type=jnp.float32,
    )
    mixed = mixed.reshape(rows_dev, 2, probe_rows, 2, NG2)
    field_real = mixed[:, 0, :, 0] - mixed[:, 1, :, 1]
    field_imag = mixed[:, 1, :, 0] + mixed[:, 0, :, 1]
    field = (
        jnp.stack([field_real, field_imag], axis=0)
        .transpose(0, 2, 1, 3)
        .reshape(2 * probe_rows, rows_dev, NG2)
    )
    field_low = field.astype(jnp.bfloat16)
    following = shifted(field_low[:, : STENCIL - 1], ("tile", "sect"), -1)
    whole = jnp.concatenate([field_low, following], axis=1).reshape(2 * probe_rows, extended * NG2)
    result = lax.dot_general(
        whole, matrix, (((1,), (1,)), ((), ())), preferred_element_type=jnp.float32
    )
    return result.reshape(2, probe_rows, rounded.shape[2])


def local_by_column(source_probes, near_blocks, bloch_angle, grid_row, grid_col, stencil, recip_kernel):
    tile_count = lax.axis_size("tile")
    sect_count = lax.axis_size("sect")
    rows_dev = NG1 // (tile_count * sect_count)
    matrix = spread_matrix(grid_row, grid_col, stencil, rows_dev)
    col_index = jnp.arange(NG2, dtype=jnp.int32)
    col_cos, col_sin = twiddle(col_index, col_index, NG2)
    col_table = jnp.concatenate([col_cos, col_sin], axis=1)
    position = jnp.arange(NG1, dtype=jnp.int32)
    forward_cos, forward_sin = twiddle(position, position, NG1)
    row_forward = jnp.concatenate([forward_cos, forward_sin], axis=0)
    inverse_cos, inverse_sin = twiddle(position, position, NG1)
    row_inverse = jnp.concatenate([inverse_cos, inverse_sin], axis=0)

    def apply_operator(source):
        rounded = source.astype(jnp.bfloat16)
        near_part = near_term(rounded, near_blocks, bloch_angle)
        recip_part = recip_term(rounded, matrix, recip_kernel, col_table, row_forward, row_inverse)
        return 0.5 * source + near_part + recip_part

    first_image = apply_operator(source_probes)
    second_image = apply_operator(first_image)
    return (first_image, second_image)


def tap_rows(row_ref, weights_ref, extended, col_off):
    panels = row_ref.shape[-1]
    place = lax.broadcasted_iota(jnp.int32, (extended, panels), 0)
    values = jnp.zeros((extended, panels), jnp.float32)
    for row_off in range(STENCIL):
        tap = row_off * STENCIL + col_off
        hit = place == row_ref[0] + row_off
        values = jnp.where(hit, weights_ref[0, tap : tap + 1], values)
    return values


def one_hot(column_ref):
    panels = column_ref.shape[-1]
    cells = lax.broadcasted_iota(jnp.int32, (NG2, panels), 0)
    return jnp.where(cells == column_ref[0], 1.0, 0.0).astype(jnp.bfloat16)


def spread_kernel(values_ref, row_ref, column_ref, weights_ref, grid_ref, left_ref):
    extended = grid_ref.shape[2]
    for col_off in range(STENCIL):
        taps = tap_rows(row_ref, weights_ref, extended, col_off)
        parts = jnp.concatenate([taps * values_ref[0, c : c + 1] for c in range(2)], axis=0)
        high = parts.astype(jnp.bfloat16)
        left_ref[2 * col_off] = high
        left_ref[2 * col_off + 1] = (parts - high.astype(jnp.float32)).astype(jnp.bfloat16)
    count, rows, panels = left_ref.shape
    placed = lax.dot_general(
        left_ref[...].reshape(count * rows, panels),
        one_hot(column_ref),
        (((1,), (1,)), ((), ())),
        preferred_element_type=jnp.float32,
    ).reshape(STENCIL, 2, rows, NG2)
    grid = placed[0, 0] + placed[0, 1]
    for col_off in range(1, STENCIL):
        grid = grid + pltpu.roll(placed[col_off, 0] + placed[col_off, 1], col_off, 1)
    grid_ref[...] = grid.reshape(grid_ref.shape)


def spread(values, local_row, column, weights, extended):
    blocks, _, panels = local_row.shape
    return pl.pallas_call(
        spread_kernel,
        grid=(blocks,),
        in_specs=[
            pl.BlockSpec((1, 2, panels), lambda b: (b, 0, 0)),
            pl.BlockSpec((1, 1, panels), lambda b: (b, 0, 0)),
            pl.BlockSpec((1, 1, panels), lambda b: (b, 0, 0)),
            pl.BlockSpec((1, STENCIL * STENCIL, panels), lambda b: (b, 0, 0)),
        ],
        out_specs=pl.BlockSpec((2, 1, extended, NG2), lambda b: (0, b, 0, 0)),
        out_shape=jax.ShapeDtypeStruct((2, blocks, extended, NG2), jnp.float32),
        scratch_shapes=[pltpu.VMEM((2 * STENCIL, 2 * extended, panels), jnp.bfloat16)],
        compiler_params=pltpu.CompilerParams(vmem_limit_bytes=24 << 20),
    )(values, local_row, column, weights)


def take_kernel(field_ref, row_ref, column_ref, weights_ref, out_ref, left_ref):
    extended = field_ref.shape[2]
    count, rows, _ = left_ref.shape
    panels = row_ref.shape[-1]
    field = field_ref[...].reshape(rows, NG2)
    left_ref[0] = field.astype(jnp.bfloat16)
    for col_off in range(1, count):
        left_ref[col_off] = pltpu.roll(field, NG2 - col_off, 1).astype(jnp.bfloat16)
    taken = jnp.dot(
        left_ref[...].reshape(count * rows, NG2),
        one_hot(column_ref),
        preferred_element_type=jnp.float32,
    ).reshape(count, 2, extended, panels)
    total = [jnp.zeros((extended, panels), jnp.float32) for _ in range(2)]
    for col_off in range(count):
        taps = tap_rows(row_ref, weights_ref, extended, col_off)
        total = [total[c] + taps * taken[col_off, c] for c in range(2)]
    out_ref[0] = jnp.concatenate([jnp.sum(t, axis=0, keepdims=True) for t in total], axis=0)


def take(field, local_row, column, weights):
    _, blocks, extended, _ = field.shape
    panels = local_row.shape[-1]
    return pl.pallas_call(
        take_kernel,
        grid=(blocks,),
        in_specs=[
            pl.BlockSpec((2, 1, extended, NG2), lambda b: (0, b, 0, 0)),
            pl.BlockSpec((1, 1, panels), lambda b: (b, 0, 0)),
            pl.BlockSpec((1, 1, panels), lambda b: (b, 0, 0)),
            pl.BlockSpec((1, STENCIL * STENCIL, panels), lambda b: (b, 0, 0)),
        ],
        out_specs=pl.BlockSpec((1, 2, panels), lambda b: (b, 0, 0)),
        out_shape=jax.ShapeDtypeStruct((blocks, 2, panels), jnp.float32),
        scratch_shapes=[pltpu.VMEM((STENCIL, 2 * extended, NG2), jnp.bfloat16)],
        compiler_params=pltpu.CompilerParams(vmem_limit_bytes=24 << 20),
    )(field, local_row, column, weights)


def near_kernel(phase_ref, pieces_ref, blocks_ref, source_ref, out_ref):
    index = pl.program_id(0)
    probe_rows = source_ref.shape[1]

    @pl.when(index == 0)
    def _():
        out_ref[...] = 0.5 * source_ref[...]

    piece = pieces_ref[0]
    with_real = jnp.dot(piece, blocks_ref[0, 0], preferred_element_type=jnp.float32)
    with_imag = jnp.dot(piece, blocks_ref[1, 0], preferred_element_type=jnp.float32)
    part_real = with_real[:probe_rows] - with_imag[probe_rows:]
    part_imag = with_real[probe_rows:] + with_imag[:probe_rows]
    cos_part, sin_part = phase_ref[0, index], phase_ref[1, index]
    out_ref[0] += part_real * cos_part - part_imag * sin_part
    out_ref[1] += part_real * sin_part + part_imag * cos_part


def near_phases(bloch_angle):
    angles = []
    for tile_off in (-1, 0, 1):
        for sect_off in (-1, 0, 1):
            angle = jnp.float32(0.0)
            for axis, off, which in (("tile", tile_off, 0), ("sect", sect_off, 1)):
                if off != 0:
                    last = lax.axis_size(axis) - 1 if off == 1 else 0
                    border = lax.axis_index(axis) == last
                    angle = angle + jnp.where(border, bloch_angle[which] * off, 0.0)
            angles.append(angle)
    angles = jnp.stack(angles)
    return jnp.stack([jnp.cos(angles), jnp.sin(angles)])


def near_and_half(source, rounded, near_blocks, phases):
    _, probe_rows, panels = rounded.shape
    packed = rounded.reshape(2 * probe_rows, panels)[None]
    column = jnp.concatenate([shifted(packed, "tile", 1), packed, shifted(packed, "tile", -1)])
    pieces = jnp.stack([shifted(column, "sect", 1), column, shifted(column, "sect", -1)], axis=1)
    pieces = pieces.reshape(9, 2 * probe_rows, panels)
    return pl.pallas_call(
        near_kernel,
        grid=(9,),
        in_specs=[
            pl.BlockSpec(memory_space=pltpu.SMEM),
            pl.BlockSpec((1, 2 * probe_rows, panels), lambda e: (e, 0, 0)),
            pl.BlockSpec((2, 1, panels, panels), lambda e: (0, e, 0, 0)),
            pl.BlockSpec((2, probe_rows, panels), lambda e: (0, 0, 0)),
        ],
        out_specs=pl.BlockSpec((2, probe_rows, panels), lambda e: (0, 0, 0)),
        out_shape=jax.ShapeDtypeStruct((2, probe_rows, panels), jnp.float32),
        compiler_params=pltpu.CompilerParams(vmem_limit_bytes=16 << 20),
        cost_estimate=pl.CostEstimate(
            flops=72 * probe_rows * panels * panels,
            bytes_accessed=36 * panels * panels,
            transcendentals=0,
        ),
    )(phases, pieces, near_blocks, source)


def probe_tables(grid_row, grid_col, stencil, recip_kernel, rows_dev):
    axes = ("tile", "sect")
    blocks = lax.axis_size("tile") * lax.axis_size("sect")
    panels = grid_row.shape[0]
    taps = STENCIL * STENCIL
    packed = jnp.concatenate(
        [
            stencil.reshape(taps, panels),
            (grid_row % rows_dev).astype(jnp.bfloat16)[None],
            (grid_col // 256).astype(jnp.bfloat16)[None],
            (grid_col % 256).astype(jnp.bfloat16)[None],
        ],
        axis=0,
    )
    packed = jnp.broadcast_to(packed[None], (blocks,) + packed.shape)
    packed = lax.all_to_all(packed, axes, split_axis=0, concat_axis=0, tiled=True)
    packed = packed.astype(jnp.float32)
    local_row = packed[:, taps : taps + 1].astype(jnp.int32)
    column = packed[:, taps + 1 : taps + 2] * 256 + packed[:, taps + 2 :]
    kernel = recip_kernel.T / (NG1 * NG2)
    kernel = jnp.broadcast_to(kernel[None], (blocks,) + kernel.shape)
    kernel = lax.all_to_all(kernel, axes, split_axis=0, concat_axis=0, tiled=True)
    kernel = kernel.reshape(NG2, NG1).T
    return local_row, column.astype(jnp.int32), packed[:, :taps], kernel


def row_table(blocks, rows_dev, extended):
    place = jnp.arange(blocks * extended, dtype=jnp.int32)
    row = place % extended
    grid_row = place // extended * rows_dev + row
    used = (row < rows_dev + STENCIL - 1)[None, :]
    cos, sin = twiddle(jnp.arange(NG1, dtype=jnp.int32), grid_row, NG1)
    cos, sin = jnp.where(used, cos, 0.0), jnp.where(used, sin, 0.0)
    return jnp.concatenate(
        [jnp.concatenate([cos, sin], axis=1), jnp.concatenate([-sin, cos], axis=1)], axis=0
    )


def probe_recip(rounded, local_row, column, weights, kernel, rows, col_table, extended):
    axes = ("tile", "sect")
    probes, panels = rounded.shape[1], rounded.shape[2]
    blocks = local_row.shape[0]
    held = probes // blocks
    mine = lax.all_to_all(rounded.transpose(1, 0, 2), axes, split_axis=0, concat_axis=0, tiled=True)
    mine = mine.reshape(blocks, held, 2, panels).astype(jnp.float32)
    results = []
    for q in range(held):
        grid = spread(mine[:, q], local_row, column, weights, extended).reshape(-1, NG2)
        freq = jnp.dot(rows, grid, precision=HIGH, preferred_element_type=jnp.float32)
        freq = jnp.dot(freq, col_table, precision=HIGH, preferred_element_type=jnp.float32)
        freq_real = (freq[:NG1, :NG2] + freq[NG1:, NG2:]) * kernel
        freq_imag = (freq[NG1:, :NG2] - freq[:NG1, NG2:]) * kernel
        freq = jnp.concatenate([freq_real, freq_imag], axis=0)
        back = jnp.dot(freq, col_table, precision=HIGH, preferred_element_type=jnp.float32)
        back_real = back[:NG1, :NG2] - back[NG1:, NG2:]
        back_imag = back[NG1:, :NG2] + back[:NG1, NG2:]
        back = jnp.concatenate([back_real, back_imag], axis=0)
        field = lax.dot_general(
            rows, back, (((0,), (0,)), ((), ())), precision=HIGH, preferred_element_type=jnp.float32
        )
        field = field.reshape(2, blocks, extended, NG2)
        results.append(take(field, local_row, column, weights))
    result = jnp.stack(results, axis=1).reshape(probes, 2, panels)
    result = lax.all_to_all(result, axes, split_axis=0, concat_axis=0, tiled=True)
    return result.transpose(1, 0, 2)


def local_by_probe(
    source_probes, near_blocks, bloch_angle, grid_row, grid_col, stencil, recip_kernel
):
    blocks = lax.axis_size("tile") * lax.axis_size("sect")
    rows_dev = NG1 // blocks
    extended = -(-(rows_dev + STENCIL - 1) // 8) * 8
    tables = probe_tables(grid_row, grid_col, stencil, recip_kernel, rows_dev)
    phases = near_phases(bloch_angle)
    rows = row_table(blocks, rows_dev, extended)
    col_index = jnp.arange(NG2, dtype=jnp.int32)
    col_table = jnp.concatenate(twiddle(col_index, col_index, NG2), axis=1)
    rows, col_table = lax.optimization_barrier((rows, col_table))

    def apply_operator(source):
        rounded = source.astype(jnp.bfloat16)
        recip_part = probe_recip(rounded, *tables, rows, col_table, extended)
        return near_and_half(source, rounded, near_blocks, phases) + recip_part

    first_image = apply_operator(source_probes)
    second_image = apply_operator(first_image)
    return (first_image, second_image)


def local(source_probes, *rest):
    blocks = lax.axis_size("tile") * lax.axis_size("sect")
    if source_probes.shape[1] % blocks == 0:
        return local_by_probe(source_probes, *rest)
    return local_by_column(source_probes, *rest)


def solution(mesh):
    return jax.shard_map(
        local,
        mesh=mesh,
        in_specs=(
            P(None, "groups", ("tile", "sect")),
            P("groups", None, None, ("tile", "sect")),
            P("groups"),
            P(("tile", "sect")),
            P(("tile", "sect")),
            P(None, None, ("tile", "sect")),
            P("groups", ("tile", "sect")),
        ),
        out_specs=(P(None, "groups", ("tile", "sect")), P(None, "groups", ("tile", "sect"))),
        check_vma=False,
    )
```

```python
import math

import jax
import jax.numpy as jnp
from jax import lax
from jax.experimental import pallas as pl
from jax.experimental.pallas import tpu as pltpu
from jax.sharding import PartitionSpec as P

STENCIL = 4
NG1 = 512
NG2 = 512


HIGHEST = lax.Precision.HIGHEST
HIGH = lax.Precision.HIGH


def with_halo(cells, sides, width):
    for axis, dim in sides:
        count = lax.axis_size(axis)
        head = lax.slice_in_dim(cells, 0, width, axis=dim)
        tail = lax.slice_in_dim(cells, cells.shape[dim] - width, cells.shape[dim], axis=dim)
        cells = jnp.concatenate(
            [
                lax.ppermute(tail, axis, [(i, (i + 1) % count) for i in range(count)]),
                cells,
                lax.ppermute(head, axis, [((i + 1) % count, i) for i in range(count)]),
            ],
            axis=dim,
        )
    return cells


def shifted(array, axis, by):
    count = lax.axis_size(axis)
    return lax.ppermute(array, axis, [(i, (i + by) % count) for i in range(count)])


def twiddle(first_index, second_index, length):
    product = first_index[:, None] * second_index[None, :] % length
    phase_angle = 2.0 * math.pi / length * product.astype(jnp.float32)
    return (jnp.cos(phase_angle), jnp.sin(phase_angle))


def spread_matrix(grid_row, grid_col, stencil, rows_dev):
    panels = grid_row.shape[0]
    span = (rows_dev + STENCIL - 1) * NG2
    local_row = grid_row % rows_dev
    cells = lax.broadcasted_iota(jnp.int32, (panels, span), 1)
    matrix = jnp.zeros((panels, span), jnp.float32)
    for row_off in range(STENCIL):
        for col_off in range(STENCIL):
            target = (local_row + row_off) * NG2 + (grid_col + col_off) % NG2
            matrix = matrix + jnp.where(
                cells == target[:, None],
                stencil[row_off, col_off].astype(jnp.float32)[:, None],
                0.0,
            )
    return matrix.astype(jnp.bfloat16)


def near_term(rounded, near_blocks, bloch_angle):
    probe_rows = rounded.shape[1]
    panels = rounded.shape[2]
    packed = rounded.reshape(2 * probe_rows, 1, 1, panels)
    widened = with_halo(packed, (("tile", 1), ("sect", 2)), 1)
    tile_pos = lax.axis_index("tile")
    tile_count = lax.axis_size("tile")
    sect_pos = lax.axis_index("sect")
    sect_count = lax.axis_size("sect")
    total_real = jnp.zeros((probe_rows, panels), jnp.float32)
    total_imag = jnp.zeros((probe_rows, panels), jnp.float32)
    for tile_off in (-1, 0, 1):
        for sect_off in (-1, 0, 1):
            index = (tile_off + 1) * 3 + sect_off + 1
            piece = widened[:, tile_off + 1, sect_off + 1, :]
            with_real = jnp.dot(piece, near_blocks[0, index], preferred_element_type=jnp.float32)
            with_imag = jnp.dot(piece, near_blocks[1, index], preferred_element_type=jnp.float32)
            part_real = with_real[:probe_rows] - with_imag[probe_rows:]
            part_imag = with_real[probe_rows:] + with_imag[:probe_rows]
            if tile_off != 0 or sect_off != 0:
                phase_angle = jnp.float32(0.0)
                if tile_off != 0:
                    border = tile_pos == (tile_count - 1 if tile_off == 1 else 0)
                    phase_angle = jnp.where(border, bloch_angle[0] * tile_off, 0.0)
                if sect_off != 0:
                    border = sect_pos == (sect_count - 1 if sect_off == 1 else 0)
                    phase_angle = phase_angle + jnp.where(border, bloch_angle[1] * sect_off, 0.0)
                cos_part = jnp.cos(phase_angle)
                sin_part = jnp.sin(phase_angle)
                part_real, part_imag = (
                    part_real * cos_part - part_imag * sin_part,
                    part_real * sin_part + part_imag * cos_part,
                )
            total_real = total_real + part_real
            total_imag = total_imag + part_imag
    return jnp.stack([total_real, total_imag])


def recip_term(rounded, matrix, recip_kernel, col_table, row_forward, row_inverse):
    probe_rows = rounded.shape[1]
    extended = matrix.shape[1] // NG2
    rows_dev = extended - (STENCIL - 1)
    flat = rounded.reshape(2 * probe_rows, rounded.shape[2])
    spread = jnp.dot(flat, matrix, preferred_element_type=jnp.float32)
    spread = spread.reshape(2 * probe_rows, extended, NG2)
    overflow = spread[:, rows_dev:]
    incoming = shifted(overflow, ("tile", "sect"), 1)
    grid = jnp.concatenate(
        [spread[:, : STENCIL - 1] + incoming, spread[:, STENCIL - 1 : rows_dev]], axis=1
    )
    grid = grid.transpose(1, 0, 2).reshape(rows_dev * 2 * probe_rows, NG2)
    mixed = jnp.dot(grid, col_table, precision=HIGHEST, preferred_element_type=jnp.float32)
    mixed = mixed.reshape(rows_dev, 2, probe_rows, 2, NG2)
    spec_real = mixed[:, 0, :, 0] + mixed[:, 1, :, 1]
    spec_imag = mixed[:, 1, :, 0] - mixed[:, 0, :, 1]
    spectrum = jnp.stack([spec_real, spec_imag], axis=1).reshape(rows_dev, 2 * probe_rows, NG2)
    columns = lax.all_to_all(spectrum, ("tile", "sect"), split_axis=2, concat_axis=0, tiled=True)
    cols_dev = columns.shape[2]
    stacked = jnp.dot(
        row_forward,
        columns.reshape(NG1, 2 * probe_rows * cols_dev),
        precision=HIGHEST,
        preferred_element_type=jnp.float32,
    )
    stacked = stacked.reshape(2, NG1, 2, probe_rows, cols_dev)
    scale = recip_kernel[:, None, :] / (NG1 * NG2)
    freq_real = (stacked[0, :, 0] + stacked[1, :, 1]) * scale
    freq_imag = (stacked[0, :, 1] - stacked[1, :, 0]) * scale
    freq = jnp.stack([freq_real, freq_imag], axis=1).reshape(NG1, 2 * probe_rows * cols_dev)
    back = jnp.dot(row_inverse, freq, precision=HIGHEST, preferred_element_type=jnp.float32)
    back = back.reshape(2, NG1, 2, probe_rows, cols_dev)
    out_real = back[0, :, 0] - back[1, :, 1]
    out_imag = back[0, :, 1] + back[1, :, 0]
    spatial = jnp.stack([out_real, out_imag], axis=1).reshape(NG1, 2 * probe_rows, cols_dev)
    row_blocks = lax.all_to_all(spatial, ("tile", "sect"), split_axis=0, concat_axis=2, tiled=True)
    mixed = jnp.dot(
        row_blocks.reshape(rows_dev * 2 * probe_rows, NG2),
        col_table,
        precision=HIGHEST,
        preferred_element_type=jnp.float32,
    )
    mixed = mixed.reshape(rows_dev, 2, probe_rows, 2, NG2)
    field_real = mixed[:, 0, :, 0] - mixed[:, 1, :, 1]
    field_imag = mixed[:, 1, :, 0] + mixed[:, 0, :, 1]
    field = (
        jnp.stack([field_real, field_imag], axis=0)
        .transpose(0, 2, 1, 3)
        .reshape(2 * probe_rows, rows_dev, NG2)
    )
    field_low = field.astype(jnp.bfloat16)
    following = shifted(field_low[:, : STENCIL - 1], ("tile", "sect"), -1)
    whole = jnp.concatenate([field_low, following], axis=1).reshape(2 * probe_rows, extended * NG2)
    result = lax.dot_general(
        whole, matrix, (((1,), (1,)), ((), ())), preferred_element_type=jnp.float32
    )
    return result.reshape(2, probe_rows, rounded.shape[2])


def local_by_column(source_probes, near_blocks, bloch_angle, grid_row, grid_col, stencil, recip_kernel):
    tile_count = lax.axis_size("tile")
    sect_count = lax.axis_size("sect")
    rows_dev = NG1 // (tile_count * sect_count)
    matrix = spread_matrix(grid_row, grid_col, stencil, rows_dev)
    col_index = jnp.arange(NG2, dtype=jnp.int32)
    col_cos, col_sin = twiddle(col_index, col_index, NG2)
    col_table = jnp.concatenate([col_cos, col_sin], axis=1)
    position = jnp.arange(NG1, dtype=jnp.int32)
    forward_cos, forward_sin = twiddle(position, position, NG1)
    row_forward = jnp.concatenate([forward_cos, forward_sin], axis=0)
    inverse_cos, inverse_sin = twiddle(position, position, NG1)
    row_inverse = jnp.concatenate([inverse_cos, inverse_sin], axis=0)

    def apply_operator(source):
        rounded = source.astype(jnp.bfloat16)
        near_part = near_term(rounded, near_blocks, bloch_angle)
        recip_part = recip_term(rounded, matrix, recip_kernel, col_table, row_forward, row_inverse)
        return 0.5 * source + near_part + recip_part

    first_image = apply_operator(source_probes)
    second_image = apply_operator(first_image)
    return (first_image, second_image)


def tap_rows(row_ref, weights_ref, extended, col_off):
    panels = row_ref.shape[-1]
    place = lax.broadcasted_iota(jnp.int32, (extended, panels), 0)
    values = jnp.zeros((extended, panels), jnp.float32)
    for row_off in range(STENCIL):
        tap = row_off * STENCIL + col_off
        hit = place == row_ref[0] + row_off
        values = jnp.where(hit, weights_ref[0, tap : tap + 1], values)
    return values


def one_hot(column_ref):
    panels = column_ref.shape[-1]
    cells = lax.broadcasted_iota(jnp.int32, (NG2, panels), 0)
    return jnp.where(cells == column_ref[0], 1.0, 0.0).astype(jnp.bfloat16)


def spread_kernel(values_ref, row_ref, column_ref, weights_ref, grid_ref, left_ref):
    extended = grid_ref.shape[2]
    for col_off in range(STENCIL):
        taps = tap_rows(row_ref, weights_ref, extended, col_off)
        parts = jnp.concatenate([taps * values_ref[0, c : c + 1] for c in range(2)], axis=0)
        high = parts.astype(jnp.bfloat16)
        left_ref[2 * col_off] = high
        left_ref[2 * col_off + 1] = (parts - high.astype(jnp.float32)).astype(jnp.bfloat16)
    count, rows, panels = left_ref.shape
    placed = lax.dot_general(
        left_ref[...].reshape(count * rows, panels),
        one_hot(column_ref),
        (((1,), (1,)), ((), ())),
        preferred_element_type=jnp.float32,
    ).reshape(STENCIL, 2, rows, NG2)
    grid = placed[0, 0] + placed[0, 1]
    for col_off in range(1, STENCIL):
        grid = grid + pltpu.roll(placed[col_off, 0] + placed[col_off, 1], col_off, 1)
    grid_ref[...] = grid.reshape(grid_ref.shape)


def spread(values, local_row, column, weights, extended):
    blocks, _, panels = local_row.shape
    return pl.pallas_call(
        spread_kernel,
        grid=(blocks,),
        in_specs=[
            pl.BlockSpec((1, 2, panels), lambda b: (b, 0, 0)),
            pl.BlockSpec((1, 1, panels), lambda b: (b, 0, 0)),
            pl.BlockSpec((1, 1, panels), lambda b: (b, 0, 0)),
            pl.BlockSpec((1, STENCIL * STENCIL, panels), lambda b: (b, 0, 0)),
        ],
        out_specs=pl.BlockSpec((2, 1, extended, NG2), lambda b: (0, b, 0, 0)),
        out_shape=jax.ShapeDtypeStruct((2, blocks, extended, NG2), jnp.float32),
        scratch_shapes=[pltpu.VMEM((2 * STENCIL, 2 * extended, panels), jnp.bfloat16)],
        compiler_params=pltpu.CompilerParams(vmem_limit_bytes=24 << 20),
    )(values, local_row, column, weights)


def take_kernel(field_ref, row_ref, column_ref, weights_ref, out_ref, left_ref):
    extended = field_ref.shape[2]
    count, rows, _ = left_ref.shape
    panels = row_ref.shape[-1]
    field = field_ref[...].reshape(rows, NG2)
    left_ref[0] = field.astype(jnp.bfloat16)
    for col_off in range(1, count):
        left_ref[col_off] = pltpu.roll(field, NG2 - col_off, 1).astype(jnp.bfloat16)
    taken = jnp.dot(
        left_ref[...].reshape(count * rows, NG2),
        one_hot(column_ref),
        preferred_element_type=jnp.float32,
    ).reshape(count, 2, extended, panels)
    total = [jnp.zeros((extended, panels), jnp.float32) for _ in range(2)]
    for col_off in range(count):
        taps = tap_rows(row_ref, weights_ref, extended, col_off)
        total = [total[c] + taps * taken[col_off, c] for c in range(2)]
    out_ref[0] = jnp.concatenate([jnp.sum(t, axis=0, keepdims=True) for t in total], axis=0)


def take(field, local_row, column, weights):
    _, blocks, extended, _ = field.shape
    panels = local_row.shape[-1]
    return pl.pallas_call(
        take_kernel,
        grid=(blocks,),
        in_specs=[
            pl.BlockSpec((2, 1, extended, NG2), lambda b: (0, b, 0, 0)),
            pl.BlockSpec((1, 1, panels), lambda b: (b, 0, 0)),
            pl.BlockSpec((1, 1, panels), lambda b: (b, 0, 0)),
            pl.BlockSpec((1, STENCIL * STENCIL, panels), lambda b: (b, 0, 0)),
        ],
        out_specs=pl.BlockSpec((1, 2, panels), lambda b: (b, 0, 0)),
        out_shape=jax.ShapeDtypeStruct((blocks, 2, panels), jnp.float32),
        scratch_shapes=[pltpu.VMEM((STENCIL, 2 * extended, NG2), jnp.bfloat16)],
        compiler_params=pltpu.CompilerParams(vmem_limit_bytes=24 << 20),
    )(field, local_row, column, weights)


def near_kernel(phase_ref, pieces_ref, blocks_ref, source_ref, out_ref):
    index = pl.program_id(0)
    probe_rows = source_ref.shape[1]

    @pl.when(index == 0)
    def _():
        out_ref[...] = 0.5 * source_ref[...]

    piece = pieces_ref[0]
    with_real = jnp.dot(piece, blocks_ref[0, 0], preferred_element_type=jnp.float32)
    with_imag = jnp.dot(piece, blocks_ref[1, 0], preferred_element_type=jnp.float32)
    part_real = with_real[:probe_rows] - with_imag[probe_rows:]
    part_imag = with_real[probe_rows:] + with_imag[:probe_rows]
    cos_part, sin_part = phase_ref[0, index], phase_ref[1, index]
    out_ref[0] += part_real * cos_part - part_imag * sin_part
    out_ref[1] += part_real * sin_part + part_imag * cos_part


def near_phases(bloch_angle):
    angles = []
    for tile_off in (-1, 0, 1):
        for sect_off in (-1, 0, 1):
            angle = jnp.float32(0.0)
            for axis, off, which in (("tile", tile_off, 0), ("sect", sect_off, 1)):
                if off != 0:
                    last = lax.axis_size(axis) - 1 if off == 1 else 0
                    border = lax.axis_index(axis) == last
                    angle = angle + jnp.where(border, bloch_angle[which] * off, 0.0)
            angles.append(angle)
    angles = jnp.stack(angles)
    return jnp.stack([jnp.cos(angles), jnp.sin(angles)])


def near_and_half(source, rounded, near_blocks, phases):
    _, probe_rows, panels = rounded.shape
    packed = rounded.reshape(2 * probe_rows, panels)[None]
    column = jnp.concatenate([shifted(packed, "tile", 1), packed, shifted(packed, "tile", -1)])
    pieces = jnp.stack([shifted(column, "sect", 1), column, shifted(column, "sect", -1)], axis=1)
    pieces = pieces.reshape(9, 2 * probe_rows, panels)
    return pl.pallas_call(
        near_kernel,
        grid=(9,),
        in_specs=[
            pl.BlockSpec(memory_space=pltpu.SMEM),
            pl.BlockSpec((1, 2 * probe_rows, panels), lambda e: (e, 0, 0)),
            pl.BlockSpec((2, 1, panels, panels), lambda e: (0, e, 0, 0)),
            pl.BlockSpec((2, probe_rows, panels), lambda e: (0, 0, 0)),
        ],
        out_specs=pl.BlockSpec((2, probe_rows, panels), lambda e: (0, 0, 0)),
        out_shape=jax.ShapeDtypeStruct((2, probe_rows, panels), jnp.float32),
        compiler_params=pltpu.CompilerParams(vmem_limit_bytes=16 << 20),
        cost_estimate=pl.CostEstimate(
            flops=72 * probe_rows * panels * panels,
            bytes_accessed=36 * panels * panels,
            transcendentals=0,
        ),
    )(phases, pieces, near_blocks, source)


def pack_tables(grid_row, grid_col, stencil, rows_dev):
    panels = grid_row.shape[0]
    return jnp.concatenate(
        [
            stencil.reshape(STENCIL * STENCIL, panels),
            (grid_row % rows_dev).astype(jnp.bfloat16)[None],
            (grid_col // 256).astype(jnp.bfloat16)[None],
            (grid_col % 256).astype(jnp.bfloat16)[None],
        ],
        axis=0,
    )


def unpack_tables(packed):
    taps = STENCIL * STENCIL
    packed = packed.astype(jnp.float32)
    local_row = packed[:, taps : taps + 1].astype(jnp.int32)
    column = packed[:, taps + 1 : taps + 2] * 256 + packed[:, taps + 2 :]
    return local_row, column.astype(jnp.int32), packed[:, :taps]


def exchange(array):
    return lax.all_to_all(array, ("tile", "sect"), split_axis=0, concat_axis=0, tiled=True)


def gather_kernel(recip_kernel, blocks):
    own = recip_kernel.shape[1] // 2
    kernel = recip_kernel.T.reshape(own, 2, NG1 // 2, 2).transpose(1, 0, 3, 2)
    kernel = kernel.reshape(2 * own, NG1) / (NG1 * NG2)
    kernel = exchange(jnp.broadcast_to(kernel[None], (blocks,) + kernel.shape))
    kernel = kernel.reshape(blocks, 2, own, NG1).transpose(1, 0, 2, 3).reshape(2, NG2 // 2, NG1)
    return kernel.transpose(0, 2, 1).reshape(2, 2, NG1 // 2, NG2 // 2)


def row_table(parity, blocks, rows_dev, extended):
    place = jnp.arange(blocks // 2 * extended, dtype=jnp.int32)
    row = place % extended
    grid_row = place // extended * rows_dev + row
    used = (row < rows_dev + STENCIL - 1)[None, :]
    cos, sin = twiddle(2 * jnp.arange(NG1 // 2, dtype=jnp.int32) + parity, grid_row, NG1)
    cos, sin = jnp.where(used, cos, 0.0), jnp.where(used, sin, 0.0)
    return jnp.concatenate(
        [jnp.concatenate([cos, sin], axis=1), jnp.concatenate([-sin, cos], axis=1)], axis=0
    )


def col_tables(parity):
    place = jnp.arange(NG2 // 2, dtype=jnp.int32)
    forward = jnp.concatenate(twiddle(place, 2 * place + parity, NG2), axis=1)
    inverse = jnp.concatenate(twiddle(2 * place + parity, place, NG2), axis=1)
    return forward, inverse


def dot_high(left, right, contract=1):
    return lax.dot_general(
        left,
        right,
        (((contract,), (0,)), ((), ())),
        precision=HIGH,
        preferred_element_type=jnp.float32,
    )


def transform(grid, kernel, rows, cols):
    half_row, half_col = NG1 // 2, NG2 // 2
    places = grid.shape[1] // 2
    low, high = grid[:, :places], grid[:, places:]
    freq = jnp.concatenate(
        [
            dot_high(rows[0], (low + high).reshape(2 * places, NG2)),
            dot_high(rows[1], (low - high).reshape(2 * places, NG2)),
        ],
        axis=0,
    )
    low, high = freq[:, :half_col], freq[:, half_col:]
    halves = []
    for parity, mixed in enumerate((low + high, low - high)):
        mixed = dot_high(mixed, cols[parity][0]).reshape(2, 2, half_row, 2 * half_col)
        real = mixed[:, 0, :, :half_col] + mixed[:, 1, :, half_col:]
        imag = mixed[:, 1, :, :half_col] - mixed[:, 0, :, half_col:]
        scaled = jnp.stack([real * kernel[parity], imag * kernel[parity]], axis=1)
        mixed = dot_high(scaled.reshape(2 * NG1, half_col), cols[parity][1])
        mixed = mixed.reshape(2, 2, half_row, 2 * half_col)
        real = mixed[:, 0, :, :half_col] - mixed[:, 1, :, half_col:]
        imag = mixed[:, 1, :, :half_col] + mixed[:, 0, :, half_col:]
        halves.append(jnp.stack([real, imag], axis=1).reshape(2, NG1, half_col))
    back = jnp.concatenate([halves[0] + halves[1], halves[0] - halves[1]], axis=2)
    even = dot_high(rows[0], back[0], 0).reshape(2, places, NG2)
    odd = dot_high(rows[1], back[1], 0).reshape(2, places, NG2)
    return jnp.concatenate([even + odd, even - odd], axis=1)


def local_by_probe(
    source_probes, near_blocks, bloch_angle, grid_row, grid_col, stencil, recip_kernel
):
    blocks = lax.axis_size("tile") * lax.axis_size("sect")
    _, probes, panels = source_probes.shape
    held = probes // blocks
    rows_dev = NG1 // blocks
    extended = -(-(rows_dev + STENCIL - 1) // 8) * 8
    packed = pack_tables(grid_row, grid_col, stencil, rows_dev)
    packed = jnp.broadcast_to(packed[None], (blocks,) + packed.shape)
    first = source_probes.astype(jnp.bfloat16)
    mine = first.transpose(1, 0, 2).reshape(blocks, 2 * held, panels)
    mine = exchange(jnp.concatenate([packed, mine], axis=1))
    local_row, column, weights = unpack_tables(mine[:, : packed.shape[1]])
    mine = mine[:, packed.shape[1] :]
    kernel = gather_kernel(recip_kernel, blocks)
    phases = near_phases(bloch_angle)
    rows = [row_table(parity, blocks, rows_dev, extended) for parity in range(2)]
    cols = [col_tables(parity) for parity in range(2)]
    rows, cols = lax.optimization_barrier((rows, cols))

    def apply_operator(source, rounded, mine):
        mine = mine.reshape(blocks, held, 2, panels).astype(jnp.float32)
        results = []
        for q in range(held):
            grid = spread(mine[:, q], local_row, column, weights, extended)
            field = transform(grid.reshape(2, blocks * extended, NG2), kernel, rows, cols)
            field = field.reshape(2, blocks, extended, NG2)
            results.append(take(field, local_row, column, weights))
        result = exchange(jnp.stack(results, axis=1).reshape(probes, 2, panels))
        near = near_and_half(source, rounded, near_blocks, phases)
        return near + result.transpose(1, 0, 2)

    first_image = apply_operator(source_probes, first, mine)
    second = first_image.astype(jnp.bfloat16)
    second_image = apply_operator(first_image, second, exchange(second.transpose(1, 0, 2)))
    return (first_image, second_image)


def local(source_probes, *rest):
    blocks = lax.axis_size("tile") * lax.axis_size("sect")
    if source_probes.shape[1] % blocks == 0 and blocks % 2 == 0 and rest[-1].shape[1] % 2 == 0:
        return local_by_probe(source_probes, *rest)
    return local_by_column(source_probes, *rest)


def solution(mesh):
    return jax.shard_map(
        local,
        mesh=mesh,
        in_specs=(
            P(None, "groups", ("tile", "sect")),
            P("groups", None, None, ("tile", "sect")),
            P("groups"),
            P(("tile", "sect")),
            P(("tile", "sect")),
            P(None, None, ("tile", "sect")),
            P("groups", ("tile", "sect")),
        ),
        out_specs=(P(None, "groups", ("tile", "sect")), P(None, "groups", ("tile", "sect"))),
        check_vma=False,
    )
```

```python
import math

import jax
import jax.numpy as jnp
from jax import lax
from jax.experimental import pallas as pl
from jax.experimental.pallas import tpu as pltpu
from jax.sharding import PartitionSpec as P

STENCIL = 4
NG1 = 512
NG2 = 512


HIGHEST = lax.Precision.HIGHEST
HIGH = lax.Precision.HIGH


def with_halo(cells, sides, width):
    for axis, dim in sides:
        count = lax.axis_size(axis)
        head = lax.slice_in_dim(cells, 0, width, axis=dim)
        tail = lax.slice_in_dim(cells, cells.shape[dim] - width, cells.shape[dim], axis=dim)
        cells = jnp.concatenate(
            [
                lax.ppermute(tail, axis, [(i, (i + 1) % count) for i in range(count)]),
                cells,
                lax.ppermute(head, axis, [((i + 1) % count, i) for i in range(count)]),
            ],
            axis=dim,
        )
    return cells


def shifted(array, axis, by):
    count = lax.axis_size(axis)
    return lax.ppermute(array, axis, [(i, (i + by) % count) for i in range(count)])


def twiddle(first_index, second_index, length):
    product = first_index[:, None] * second_index[None, :] % length
    phase_angle = 2.0 * math.pi / length * product.astype(jnp.float32)
    return (jnp.cos(phase_angle), jnp.sin(phase_angle))


def spread_matrix(grid_row, grid_col, stencil, rows_dev):
    panels = grid_row.shape[0]
    span = (rows_dev + STENCIL - 1) * NG2
    local_row = grid_row % rows_dev
    cells = lax.broadcasted_iota(jnp.int32, (panels, span), 1)
    matrix = jnp.zeros((panels, span), jnp.float32)
    for row_off in range(STENCIL):
        for col_off in range(STENCIL):
            target = (local_row + row_off) * NG2 + (grid_col + col_off) % NG2
            matrix = matrix + jnp.where(
                cells == target[:, None],
                stencil[row_off, col_off].astype(jnp.float32)[:, None],
                0.0,
            )
    return matrix.astype(jnp.bfloat16)


def near_term(rounded, near_blocks, bloch_angle):
    probe_rows = rounded.shape[1]
    panels = rounded.shape[2]
    packed = rounded.reshape(2 * probe_rows, 1, 1, panels)
    widened = with_halo(packed, (("tile", 1), ("sect", 2)), 1)
    tile_pos = lax.axis_index("tile")
    tile_count = lax.axis_size("tile")
    sect_pos = lax.axis_index("sect")
    sect_count = lax.axis_size("sect")
    total_real = jnp.zeros((probe_rows, panels), jnp.float32)
    total_imag = jnp.zeros((probe_rows, panels), jnp.float32)
    for tile_off in (-1, 0, 1):
        for sect_off in (-1, 0, 1):
            index = (tile_off + 1) * 3 + sect_off + 1
            piece = widened[:, tile_off + 1, sect_off + 1, :]
            with_real = jnp.dot(piece, near_blocks[0, index], preferred_element_type=jnp.float32)
            with_imag = jnp.dot(piece, near_blocks[1, index], preferred_element_type=jnp.float32)
            part_real = with_real[:probe_rows] - with_imag[probe_rows:]
            part_imag = with_real[probe_rows:] + with_imag[:probe_rows]
            if tile_off != 0 or sect_off != 0:
                phase_angle = jnp.float32(0.0)
                if tile_off != 0:
                    border = tile_pos == (tile_count - 1 if tile_off == 1 else 0)
                    phase_angle = jnp.where(border, bloch_angle[0] * tile_off, 0.0)
                if sect_off != 0:
                    border = sect_pos == (sect_count - 1 if sect_off == 1 else 0)
                    phase_angle = phase_angle + jnp.where(border, bloch_angle[1] * sect_off, 0.0)
                cos_part = jnp.cos(phase_angle)
                sin_part = jnp.sin(phase_angle)
                part_real, part_imag = (
                    part_real * cos_part - part_imag * sin_part,
                    part_real * sin_part + part_imag * cos_part,
                )
            total_real = total_real + part_real
            total_imag = total_imag + part_imag
    return jnp.stack([total_real, total_imag])


def recip_term(rounded, matrix, recip_kernel, col_table, row_forward, row_inverse):
    probe_rows = rounded.shape[1]
    extended = matrix.shape[1] // NG2
    rows_dev = extended - (STENCIL - 1)
    flat = rounded.reshape(2 * probe_rows, rounded.shape[2])
    spread = jnp.dot(flat, matrix, preferred_element_type=jnp.float32)
    spread = spread.reshape(2 * probe_rows, extended, NG2)
    overflow = spread[:, rows_dev:]
    incoming = shifted(overflow, ("tile", "sect"), 1)
    grid = jnp.concatenate(
        [spread[:, : STENCIL - 1] + incoming, spread[:, STENCIL - 1 : rows_dev]], axis=1
    )
    grid = grid.transpose(1, 0, 2).reshape(rows_dev * 2 * probe_rows, NG2)
    mixed = jnp.dot(grid, col_table, precision=HIGHEST, preferred_element_type=jnp.float32)
    mixed = mixed.reshape(rows_dev, 2, probe_rows, 2, NG2)
    spec_real = mixed[:, 0, :, 0] + mixed[:, 1, :, 1]
    spec_imag = mixed[:, 1, :, 0] - mixed[:, 0, :, 1]
    spectrum = jnp.stack([spec_real, spec_imag], axis=1).reshape(rows_dev, 2 * probe_rows, NG2)
    columns = lax.all_to_all(spectrum, ("tile", "sect"), split_axis=2, concat_axis=0, tiled=True)
    cols_dev = columns.shape[2]
    stacked = jnp.dot(
        row_forward,
        columns.reshape(NG1, 2 * probe_rows * cols_dev),
        precision=HIGHEST,
        preferred_element_type=jnp.float32,
    )
    stacked = stacked.reshape(2, NG1, 2, probe_rows, cols_dev)
    scale = recip_kernel[:, None, :] / (NG1 * NG2)
    freq_real = (stacked[0, :, 0] + stacked[1, :, 1]) * scale
    freq_imag = (stacked[0, :, 1] - stacked[1, :, 0]) * scale
    freq = jnp.stack([freq_real, freq_imag], axis=1).reshape(NG1, 2 * probe_rows * cols_dev)
    back = jnp.dot(row_inverse, freq, precision=HIGHEST, preferred_element_type=jnp.float32)
    back = back.reshape(2, NG1, 2, probe_rows, cols_dev)
    out_real = back[0, :, 0] - back[1, :, 1]
    out_imag = back[0, :, 1] + back[1, :, 0]
    spatial = jnp.stack([out_real, out_imag], axis=1).reshape(NG1, 2 * probe_rows, cols_dev)
    row_blocks = lax.all_to_all(spatial, ("tile", "sect"), split_axis=0, concat_axis=2, tiled=True)
    mixed = jnp.dot(
        row_blocks.reshape(rows_dev * 2 * probe_rows, NG2),
        col_table,
        precision=HIGHEST,
        preferred_element_type=jnp.float32,
    )
    mixed = mixed.reshape(rows_dev, 2, probe_rows, 2, NG2)
    field_real = mixed[:, 0, :, 0] - mixed[:, 1, :, 1]
    field_imag = mixed[:, 1, :, 0] + mixed[:, 0, :, 1]
    field = (
        jnp.stack([field_real, field_imag], axis=0)
        .transpose(0, 2, 1, 3)
        .reshape(2 * probe_rows, rows_dev, NG2)
    )
    field_low = field.astype(jnp.bfloat16)
    following = shifted(field_low[:, : STENCIL - 1], ("tile", "sect"), -1)
    whole = jnp.concatenate([field_low, following], axis=1).reshape(2 * probe_rows, extended * NG2)
    result = lax.dot_general(
        whole, matrix, (((1,), (1,)), ((), ())), preferred_element_type=jnp.float32
    )
    return result.reshape(2, probe_rows, rounded.shape[2])


def local_by_column(source_probes, near_blocks, bloch_angle, grid_row, grid_col, stencil, recip_kernel):
    tile_count = lax.axis_size("tile")
    sect_count = lax.axis_size("sect")
    rows_dev = NG1 // (tile_count * sect_count)
    matrix = spread_matrix(grid_row, grid_col, stencil, rows_dev)
    col_index = jnp.arange(NG2, dtype=jnp.int32)
    col_cos, col_sin = twiddle(col_index, col_index, NG2)
    col_table = jnp.concatenate([col_cos, col_sin], axis=1)
    position = jnp.arange(NG1, dtype=jnp.int32)
    forward_cos, forward_sin = twiddle(position, position, NG1)
    row_forward = jnp.concatenate([forward_cos, forward_sin], axis=0)
    inverse_cos, inverse_sin = twiddle(position, position, NG1)
    row_inverse = jnp.concatenate([inverse_cos, inverse_sin], axis=0)

    def apply_operator(source):
        rounded = source.astype(jnp.bfloat16)
        near_part = near_term(rounded, near_blocks, bloch_angle)
        recip_part = recip_term(rounded, matrix, recip_kernel, col_table, row_forward, row_inverse)
        return 0.5 * source + near_part + recip_part

    first_image = apply_operator(source_probes)
    second_image = apply_operator(first_image)
    return (first_image, second_image)


def tap_rows(row_ref, weights_ref, extended, col_off):
    panels = row_ref.shape[-1]
    place = lax.broadcasted_iota(jnp.int32, (extended, panels), 0)
    values = jnp.zeros((extended, panels), jnp.float32)
    for row_off in range(STENCIL):
        tap = row_off * STENCIL + col_off
        hit = place == row_ref[0] + row_off
        values = jnp.where(hit, weights_ref[0, tap : tap + 1], values)
    return values


def one_hot(column_ref):
    panels = column_ref.shape[-1]
    cells = lax.broadcasted_iota(jnp.int32, (NG2, panels), 0)
    return jnp.where(cells == column_ref[0], 1.0, 0.0).astype(jnp.bfloat16)


def spread_kernel(values_ref, row_ref, column_ref, weights_ref, grid_ref, left_ref):
    extended = grid_ref.shape[2]
    for col_off in range(STENCIL):
        taps = tap_rows(row_ref, weights_ref, extended, col_off)
        parts = jnp.concatenate([taps * values_ref[0, c : c + 1] for c in range(2)], axis=0)
        high = parts.astype(jnp.bfloat16)
        left_ref[2 * col_off] = high
        left_ref[2 * col_off + 1] = (parts - high.astype(jnp.float32)).astype(jnp.bfloat16)
    count, rows, panels = left_ref.shape
    placed = lax.dot_general(
        left_ref[...].reshape(count * rows, panels),
        one_hot(column_ref),
        (((1,), (1,)), ((), ())),
        preferred_element_type=jnp.float32,
    ).reshape(STENCIL, 2, rows, NG2)
    grid = placed[0, 0] + placed[0, 1]
    for col_off in range(1, STENCIL):
        grid = grid + pltpu.roll(placed[col_off, 0] + placed[col_off, 1], col_off, 1)
    grid_ref[...] = grid.reshape(grid_ref.shape)


def spread(values, local_row, column, weights, extended):
    blocks, _, panels = local_row.shape
    return pl.pallas_call(
        spread_kernel,
        grid=(blocks,),
        in_specs=[
            pl.BlockSpec((1, 2, panels), lambda b: (b, 0, 0)),
            pl.BlockSpec((1, 1, panels), lambda b: (b, 0, 0)),
            pl.BlockSpec((1, 1, panels), lambda b: (b, 0, 0)),
            pl.BlockSpec((1, STENCIL * STENCIL, panels), lambda b: (b, 0, 0)),
        ],
        out_specs=pl.BlockSpec((2, 1, extended, NG2), lambda b: (0, b, 0, 0)),
        out_shape=jax.ShapeDtypeStruct((2, blocks, extended, NG2), jnp.float32),
        scratch_shapes=[pltpu.VMEM((2 * STENCIL, 2 * extended, panels), jnp.bfloat16)],
        compiler_params=pltpu.CompilerParams(vmem_limit_bytes=24 << 20),
    )(values, local_row, column, weights)


def take_kernel(field_ref, row_ref, column_ref, weights_ref, out_ref, left_ref):
    extended = field_ref.shape[2]
    count, rows, _ = left_ref.shape
    panels = row_ref.shape[-1]
    field = field_ref[...].reshape(rows, NG2)
    left_ref[0] = field.astype(jnp.bfloat16)
    for col_off in range(1, count):
        left_ref[col_off] = pltpu.roll(field, NG2 - col_off, 1).astype(jnp.bfloat16)
    taken = jnp.dot(
        left_ref[...].reshape(count * rows, NG2),
        one_hot(column_ref),
        preferred_element_type=jnp.float32,
    ).reshape(count, 2, extended, panels)
    total = [jnp.zeros((extended, panels), jnp.float32) for _ in range(2)]
    for col_off in range(count):
        taps = tap_rows(row_ref, weights_ref, extended, col_off)
        total = [total[c] + taps * taken[col_off, c] for c in range(2)]
    out_ref[0] = jnp.concatenate([jnp.sum(t, axis=0, keepdims=True) for t in total], axis=0)


def take(field, local_row, column, weights):
    _, blocks, extended, _ = field.shape
    panels = local_row.shape[-1]
    return pl.pallas_call(
        take_kernel,
        grid=(blocks,),
        in_specs=[
            pl.BlockSpec((2, 1, extended, NG2), lambda b: (0, b, 0, 0)),
            pl.BlockSpec((1, 1, panels), lambda b: (b, 0, 0)),
            pl.BlockSpec((1, 1, panels), lambda b: (b, 0, 0)),
            pl.BlockSpec((1, STENCIL * STENCIL, panels), lambda b: (b, 0, 0)),
        ],
        out_specs=pl.BlockSpec((1, 2, panels), lambda b: (b, 0, 0)),
        out_shape=jax.ShapeDtypeStruct((blocks, 2, panels), jnp.float32),
        scratch_shapes=[pltpu.VMEM((STENCIL, 2 * extended, NG2), jnp.bfloat16)],
        compiler_params=pltpu.CompilerParams(vmem_limit_bytes=24 << 20),
    )(field, local_row, column, weights)


def near_kernel(phase_ref, pieces_ref, blocks_ref, source_ref, out_ref):
    index = pl.program_id(0)
    probe_rows = source_ref.shape[1]

    @pl.when(index == 0)
    def _():
        out_ref[...] = 0.5 * source_ref[...]

    piece = pieces_ref[0]
    with_real = jnp.dot(piece, blocks_ref[0, 0], preferred_element_type=jnp.float32)
    with_imag = jnp.dot(piece, blocks_ref[1, 0], preferred_element_type=jnp.float32)
    part_real = with_real[:probe_rows] - with_imag[probe_rows:]
    part_imag = with_real[probe_rows:] + with_imag[:probe_rows]
    cos_part, sin_part = phase_ref[0, index], phase_ref[1, index]
    out_ref[0] += part_real * cos_part - part_imag * sin_part
    out_ref[1] += part_real * sin_part + part_imag * cos_part


def near_phases(bloch_angle):
    angles = []
    for tile_off in (-1, 0, 1):
        for sect_off in (-1, 0, 1):
            angle = jnp.float32(0.0)
            for axis, off, which in (("tile", tile_off, 0), ("sect", sect_off, 1)):
                if off != 0:
                    last = lax.axis_size(axis) - 1 if off == 1 else 0
                    border = lax.axis_index(axis) == last
                    angle = angle + jnp.where(border, bloch_angle[which] * off, 0.0)
            angles.append(angle)
    angles = jnp.stack(angles)
    return jnp.stack([jnp.cos(angles), jnp.sin(angles)])


def near_and_half(source, rounded, near_blocks, phases):
    _, probe_rows, panels = rounded.shape
    packed = rounded.reshape(2 * probe_rows, panels)[None]
    column = jnp.concatenate([shifted(packed, "tile", 1), packed, shifted(packed, "tile", -1)])
    pieces = jnp.stack([shifted(column, "sect", 1), column, shifted(column, "sect", -1)], axis=1)
    pieces = pieces.reshape(9, 2 * probe_rows, panels)
    return pl.pallas_call(
        near_kernel,
        grid=(9,),
        in_specs=[
            pl.BlockSpec(memory_space=pltpu.SMEM),
            pl.BlockSpec((1, 2 * probe_rows, panels), lambda e: (e, 0, 0)),
            pl.BlockSpec((2, 1, panels, panels), lambda e: (0, e, 0, 0)),
            pl.BlockSpec((2, probe_rows, panels), lambda e: (0, 0, 0)),
        ],
        out_specs=pl.BlockSpec((2, probe_rows, panels), lambda e: (0, 0, 0)),
        out_shape=jax.ShapeDtypeStruct((2, probe_rows, panels), jnp.float32),
        compiler_params=pltpu.CompilerParams(vmem_limit_bytes=16 << 20),
        cost_estimate=pl.CostEstimate(
            flops=72 * probe_rows * panels * panels,
            bytes_accessed=36 * panels * panels,
            transcendentals=0,
        ),
    )(phases, pieces, near_blocks, source)


def pack_tables(grid_row, grid_col, stencil, rows_dev):
    panels = grid_row.shape[0]
    return jnp.concatenate(
        [
            stencil.reshape(STENCIL * STENCIL, panels),
            (grid_row % rows_dev).astype(jnp.bfloat16)[None],
            (grid_col // 256).astype(jnp.bfloat16)[None],
            (grid_col % 256).astype(jnp.bfloat16)[None],
        ],
        axis=0,
    )


def unpack_tables(packed):
    taps = STENCIL * STENCIL
    packed = packed.astype(jnp.float32)
    local_row = packed[:, taps : taps + 1].astype(jnp.int32)
    column = packed[:, taps + 1 : taps + 2] * 256 + packed[:, taps + 2 :]
    return local_row, column.astype(jnp.int32), packed[:, :taps]


def exchange(array):
    return lax.all_to_all(array, ("tile", "sect"), split_axis=0, concat_axis=0, tiled=True)


def even_then_odd(length):
    place = jnp.arange(length, dtype=jnp.int32)
    source = place % (length // 2) * 2 + place // (length // 2)
    return (source[:, None] == place[None, :]).astype(jnp.float32)


def gather_kernel(recip_kernel, blocks):
    own = recip_kernel.shape[1] // 2
    kernel = lax.dot_general(
        recip_kernel / (NG1 * NG2),
        even_then_odd(NG1),
        (((0,), (1,)), ((), ())),
        precision=HIGHEST,
        preferred_element_type=jnp.float32,
    )
    kernel = jnp.dot(
        even_then_odd(2 * own), kernel, precision=HIGHEST, preferred_element_type=jnp.float32
    )
    kernel = exchange(jnp.broadcast_to(kernel[None], (blocks,) + kernel.shape))
    kernel = kernel.reshape(blocks, 2, own, NG1).transpose(1, 0, 2, 3).reshape(2, NG2 // 2, NG1)
    return kernel.transpose(0, 2, 1).reshape(2, 2, NG1 // 2, NG2 // 2)


def row_table(parity, blocks, rows_dev, extended):
    place = jnp.arange(blocks // 2 * extended, dtype=jnp.int32)
    row = place % extended
    grid_row = place // extended * rows_dev + row
    used = (row < rows_dev + STENCIL - 1)[None, :]
    cos, sin = twiddle(2 * jnp.arange(NG1 // 2, dtype=jnp.int32) + parity, grid_row, NG1)
    cos, sin = jnp.where(used, cos, 0.0), jnp.where(used, sin, 0.0)
    return jnp.concatenate(
        [jnp.concatenate([cos, sin], axis=1), jnp.concatenate([-sin, cos], axis=1)], axis=0
    )


def col_tables(parity):
    place = jnp.arange(NG2 // 2, dtype=jnp.int32)
    forward = jnp.concatenate(twiddle(place, 2 * place + parity, NG2), axis=1)
    inverse = jnp.concatenate(twiddle(2 * place + parity, place, NG2), axis=1)
    return forward, inverse


def dot_high(left, right, contract=1):
    return lax.dot_general(
        left,
        right,
        (((contract,), (0,)), ((), ())),
        precision=HIGH,
        preferred_element_type=jnp.float32,
    )


def transform(grid, kernel, rows, cols):
    half_row, half_col = NG1 // 2, NG2 // 2
    places = grid.shape[1] // 2
    low, high = grid[:, :places], grid[:, places:]
    freq = jnp.concatenate(
        [
            dot_high(rows[0], (low + high).reshape(2 * places, NG2)),
            dot_high(rows[1], (low - high).reshape(2 * places, NG2)),
        ],
        axis=0,
    )
    low, high = freq[:, :half_col], freq[:, half_col:]
    halves = []
    for parity, mixed in enumerate((low + high, low - high)):
        mixed = dot_high(mixed, cols[parity][0]).reshape(2, 2, half_row, 2 * half_col)
        real = mixed[:, 0, :, :half_col] + mixed[:, 1, :, half_col:]
        imag = mixed[:, 1, :, :half_col] - mixed[:, 0, :, half_col:]
        scaled = jnp.stack([real * kernel[parity], imag * kernel[parity]], axis=1)
        mixed = dot_high(scaled.reshape(2 * NG1, half_col), cols[parity][1])
        mixed = mixed.reshape(2, 2, half_row, 2 * half_col)
        real = mixed[:, 0, :, :half_col] - mixed[:, 1, :, half_col:]
        imag = mixed[:, 1, :, :half_col] + mixed[:, 0, :, half_col:]
        halves.append(jnp.stack([real, imag], axis=1).reshape(2, NG1, half_col))
    back = jnp.concatenate([halves[0] + halves[1], halves[0] - halves[1]], axis=2)
    even = dot_high(rows[0], back[0], 0).reshape(2, places, NG2)
    odd = dot_high(rows[1], back[1], 0).reshape(2, places, NG2)
    return jnp.concatenate([even + odd, even - odd], axis=1)


def local_by_probe(
    source_probes, near_blocks, bloch_angle, grid_row, grid_col, stencil, recip_kernel
):
    blocks = lax.axis_size("tile") * lax.axis_size("sect")
    _, probes, panels = source_probes.shape
    held = probes // blocks
    rows_dev = NG1 // blocks
    extended = -(-(rows_dev + STENCIL - 1) // 8) * 8
    packed = pack_tables(grid_row, grid_col, stencil, rows_dev)
    packed = jnp.broadcast_to(packed[None], (blocks,) + packed.shape)
    first = source_probes.astype(jnp.bfloat16)
    mine = first.transpose(1, 0, 2).reshape(blocks, 2 * held, panels)
    mine = exchange(jnp.concatenate([packed, mine], axis=1))
    local_row, column, weights = unpack_tables(mine[:, : packed.shape[1]])
    mine = mine[:, packed.shape[1] :]
    kernel = gather_kernel(recip_kernel, blocks)
    phases = near_phases(bloch_angle)
    rows = [row_table(parity, blocks, rows_dev, extended) for parity in range(2)]
    cols = [col_tables(parity) for parity in range(2)]
    rows, cols = lax.optimization_barrier((rows, cols))

    def apply_operator(source, rounded, mine):
        mine = mine.reshape(blocks, held, 2, panels).astype(jnp.float32)
        results = []
        for q in range(held):
            grid = spread(mine[:, q], local_row, column, weights, extended)
            field = transform(grid.reshape(2, blocks * extended, NG2), kernel, rows, cols)
            field = field.reshape(2, blocks, extended, NG2)
            results.append(take(field, local_row, column, weights))
        result = exchange(jnp.stack(results, axis=1).reshape(probes, 2, panels))
        near = near_and_half(source, rounded, near_blocks, phases)
        return near + result.transpose(1, 0, 2)

    first_image = apply_operator(source_probes, first, mine)
    second = first_image.astype(jnp.bfloat16)
    second_image = apply_operator(first_image, second, exchange(second.transpose(1, 0, 2)))
    return (first_image, second_image)


def local(source_probes, *rest):
    blocks = lax.axis_size("tile") * lax.axis_size("sect")
    if source_probes.shape[1] % blocks == 0 and blocks % 2 == 0 and rest[-1].shape[1] % 2 == 0:
        return local_by_probe(source_probes, *rest)
    return local_by_column(source_probes, *rest)


def solution(mesh):
    return jax.shard_map(
        local,
        mesh=mesh,
        in_specs=(
            P(None, "groups", ("tile", "sect")),
            P("groups", None, None, ("tile", "sect")),
            P("groups"),
            P(("tile", "sect")),
            P(("tile", "sect")),
            P(None, None, ("tile", "sect")),
            P("groups", ("tile", "sect")),
        ),
        out_specs=(P(None, "groups", ("tile", "sect")), P(None, "groups", ("tile", "sect"))),
        check_vma=False,
    )
```
